32 devices in a mesh: frame: 8 (over y, x, core), space: 4 (over z).
Axes of the slice: x: 2, y: 2, z: 4, core: 2. Of those that a mesh axis runs over, the one named last changes fastest.
Arguments:
- query_vectors: bfloat16 [32, 12, 12, 1024], P('frame', 'space'), may hold values from -6 to 6
- key_vectors: bfloat16 [32, 12, 12, 1024], P('frame', 'space'), may hold values from -6 to 6
- value_vectors: bfloat16 [32, 12, 12, 1024], P('frame', 'space'), may hold values from -6 to 6
- out_cotangent: bfloat16 [32, 12, 12, 1024], P('frame', 'space'), may hold values from -6 to 6
- partner_mask: int32 [32, 3], replicated, may hold values 0 or 1
Outputs:
- attended: bfloat16 [32, 12, 12, 1024], P('frame', 'space')
- query_grad: bfloat16 [32, 12, 12, 1024], P('frame', 'space')
- key_grad: bfloat16 [32, 12, 12, 1024], P('frame', 'space')
- value_grad: bfloat16 [32, 12, 12, 1024], P('frame', 'space')
The draws below stay inside these ranges and needn't reach their ends.
All inputs are finite; a program needn't handle non-finite values.
Results may differ from the reference program's by a relative error of at most 0.011.
Values may be sent and summed in bfloat16 or wider, within the bound.
No kernel may reach another device: no remote copies, remote signals or barrier semaphores. Data moves between devices by JAX's collectives and lax.ppermute only.
A program may use at most 128 MiB of HBM per device.

```python
import jax
import jax.numpy as jnp
from jax import lax

HEADS = 16
HEAD_DIM = 64
ROWS = 12
COLS = 12
FR_DEV = 4
D = 1024
FRAMES = 32
PARTNERS = 3
N_FRAME = 8


def base_field(key):
    shape = (FRAMES, ROWS, COLS, HEADS * HEAD_DIM)
    return jnp.clip(jax.random.normal(key, shape, jnp.float32), -6.0, 6.0)


def draw_query_vectors(key, part):
    field = base_field(jax.random.fold_in(key, 1))
    return field.astype(jnp.bfloat16)


def draw_key_vectors(key, part):
    field = base_field(jax.random.fold_in(key, 2))
    return field.astype(jnp.bfloat16)


def set_ends(entries, own_key, low, top_value):
    longest = entries.shape.index(max(entries.shape))
    spots = []
    for shift in (0, 1):
        where = [jax.random.randint(jax.random.fold_in(own_key, axis), (), 0, length) for axis, length in enumerate(entries.shape)]
        where[longest] = (where[longest] + shift) % entries.shape[longest]
        spots.append(tuple(where))
    return entries.at[spots[0]].set(low).at[spots[1]].set(top_value)


def block_scale(rng, shape, pieces, low, largest):
    gain = 1.0
    for axis_at, shards_of in pieces:
        draws = jax.random.uniform(jax.random.fold_in(jax.random.fold_in(rng, 6), axis_at), (shards_of,), jnp.float32, low / len(pieces), largest / len(pieces))
        gain = gain * jnp.repeat(jnp.exp(draws), shape[axis_at] // shards_of).reshape((-1,) + (1,) * (len(shape) - 1 - axis_at))
    return gain


def centred(rng, shape, deviation, most, shards=(), kind=jnp.bfloat16):
    values = deviation * jax.random.normal(rng, shape, jnp.float32)
    if shards:
        values = values * block_scale(rng, shape, shards, -0.22, 0.18)
    return jnp.clip(values, -most, most).astype(kind)


def setup_inputs(seed: int = 0) -> dict:
    splits = jax.random.split(jax.random.key(seed), 6)
    return {
        "query_vectors": draw_query_vectors(jax.random.fold_in(splits[5], 71), 0),
        "key_vectors": draw_key_vectors(jax.random.fold_in(splits[5], 71), 0),
        "value_vectors": centred(splits[2], (FRAMES, ROWS, COLS, D), 1.0, 6.0, ((0, 8), (1, 4))),
        "out_cotangent": centred(splits[3], (FRAMES, ROWS, COLS, D), 1.0, 6.0, ((0, 8), (1, 4))),
        "partner_mask": set_ends((jax.random.randint(splits[4], (FRAMES, PARTNERS), 0, 4) < 3).astype(jnp.int32), jax.random.fold_in(splits[4], 1), 0, 1),
    }


SCALE = 0.125
NEG = -1.0e30


def partners(group):
    return jnp.stack([group] + [jnp.bitwise_xor(group, 1 << which_bit) for which_bit in range(PARTNERS)]).astype(jnp.int32)


def windows(blockwise):
    padded = jnp.pad(blockwise, ((0, 0), (0, 0), (1, 1), (0, 0), (0, 0)))
    stacked = jnp.stack([padded[:, :, start:start + 3] for start in range(ROWS)])
    return stacked.reshape(ROWS, -1, blockwise.shape[-1])


def reference(query_vectors, key_vectors, value_vectors, out_cotangent, partner_mask):
    width = HEADS * HEAD_DIM
    blocks = PARTNERS + 1
    queries5 = query_vectors.reshape(N_FRAME, FR_DEV, ROWS, COLS, width)
    keys5 = key_vectors.reshape(N_FRAME, FR_DEV, ROWS, COLS, width)
    values5 = value_vectors.reshape(N_FRAME, FR_DEV, ROWS, COLS, width)
    grads5 = out_cotangent.reshape(N_FRAME, FR_DEV, ROWS, COLS, width)
    masks = partner_mask.reshape(N_FRAME, FR_DEV, PARTNERS) == 1
    near_rows = jnp.arange(ROWS)[:, None] + jnp.arange(3)[None, :] - 1
    row_valid = (near_rows >= 0) & (near_rows < ROWS)

    def own_rows(array):
        return array.transpose(1, 0, 2, 3).reshape(ROWS, -1, HEADS, HEAD_DIM).astype(jnp.float32)

    def forward_block(group):
        members = partners(group)
        key_win = windows(keys5[members]).reshape(ROWS, -1, HEADS, HEAD_DIM).astype(jnp.float32)
        value_win = windows(values5[members]).reshape(ROWS, -1, HEADS, HEAD_DIM).astype(jnp.float32)
        query_now = own_rows(queries5[group])
        grad_now = own_rows(grads5[group])
        block_ok = jnp.concatenate([jnp.ones((FR_DEV, 1), bool), masks[group]], axis=1)
        allowed = block_ok[None, :, None, :, None, None, None] & row_valid[:, None, None, None, None, :, None]
        allowed = jnp.broadcast_to(allowed, (ROWS, FR_DEV, COLS, blocks, FR_DEV, 3, COLS)).reshape(ROWS, FR_DEV * COLS, -1)
        scores = jnp.einsum("rqhe,rkhe->rhqk", query_now, key_win) * SCALE
        masked = jnp.where(allowed[:, None], scores, NEG)
        top = jnp.max(masked, axis=3, keepdims=True)
        total = jnp.sum(jnp.exp(masked - top), axis=3, keepdims=True)
        log_total = top + jnp.log(total)
        probs = jnp.exp(masked - log_total)
        weights = lax.optimization_barrier(probs.astype(jnp.bfloat16))
        attended = jnp.einsum("rhqk,rkhe->rqhe", weights.astype(jnp.float32), value_win).astype(jnp.bfloat16)
        attended = lax.optimization_barrier(attended)
        delta = jnp.sum(grad_now * attended.astype(jnp.float32), axis=3)
        grad_probs = jnp.einsum("rqhe,rkhe->rhqk", grad_now, value_win)
        grad_scores = (probs * (grad_probs - delta.transpose(0, 2, 1)[..., None])).astype(jnp.bfloat16)
        grad_scores = lax.optimization_barrier(grad_scores)
        query_grad = (jnp.einsum("rhqk,rkhe->rqhe", grad_scores.astype(jnp.float32), key_win) * SCALE).astype(jnp.bfloat16)
        lse = log_total[..., 0].transpose(0, 2, 1).reshape(ROWS, FR_DEV, COLS, HEADS).transpose(1, 0, 2, 3)
        delta_out = delta.reshape(ROWS, FR_DEV, COLS, HEADS).transpose(1, 0, 2, 3)
        attended = attended.reshape(ROWS, FR_DEV, COLS, width).transpose(1, 0, 2, 3)
        query_grad = query_grad.reshape(ROWS, FR_DEV, COLS, width).transpose(1, 0, 2, 3)
        return attended, query_grad, lse, delta_out

    groups = jnp.arange(N_FRAME, dtype=jnp.int32)
    attended, query_grad, lse_all, delta_all = lax.map(forward_block, groups)

    def backward_block(group):
        members = partners(group)
        query_win = windows(queries5[members]).reshape(ROWS, -1, HEADS, HEAD_DIM).astype(jnp.float32)
        grad_win = windows(grads5[members]).reshape(ROWS, -1, HEADS, HEAD_DIM).astype(jnp.float32)
        lse_win = windows(lse_all[members]).reshape(ROWS, -1, HEADS)
        delta_win = windows(delta_all[members]).reshape(ROWS, -1, HEADS)
        key_now = own_rows(keys5[group])
        value_now = own_rows(values5[group])
        partner_ok = jnp.stack([jnp.ones((FR_DEV,), bool)] + [masks[members[1 + which_bit]][:, which_bit] for which_bit in range(PARTNERS)])
        allowed = partner_ok[None, :, :, None, None, None, None] & row_valid[:, None, None, :, None, None, None]
        allowed = jnp.broadcast_to(allowed, (ROWS, blocks, FR_DEV, 3, COLS, FR_DEV, COLS)).reshape(ROWS, -1, FR_DEV * COLS)
        scores = jnp.einsum("rqhe,rkhe->rhqk", query_win, key_now) * SCALE
        probs = jnp.exp(jnp.where(allowed[:, None], scores - lse_win.transpose(0, 2, 1)[..., None], NEG))
        weights = lax.optimization_barrier(probs.astype(jnp.bfloat16))
        value_grad = jnp.einsum("rhqk,rqhe->rkhe", weights.astype(jnp.float32), grad_win).astype(jnp.bfloat16)
        grad_probs = jnp.einsum("rqhe,rkhe->rhqk", grad_win, value_now)
        grad_scores = (probs * (grad_probs - delta_win.transpose(0, 2, 1)[..., None])).astype(jnp.bfloat16)
        grad_scores = lax.optimization_barrier(grad_scores)
        key_grad = (jnp.einsum("rhqk,rqhe->rkhe", grad_scores.astype(jnp.float32), query_win) * SCALE).astype(jnp.bfloat16)
        key_grad = key_grad.reshape(ROWS, FR_DEV, COLS, width).transpose(1, 0, 2, 3)
        value_grad = value_grad.reshape(ROWS, FR_DEV, COLS, width).transpose(1, 0, 2, 3)
        return key_grad, value_grad

    key_grad, value_grad = lax.map(backward_block, groups)
    full = (FRAMES, ROWS, COLS, width)
    return (attended.reshape(full), query_grad.reshape(full), key_grad.reshape(full), value_grad.reshape(full))
```

```python
import functools

import jax
import jax.numpy as jnp
from jax import lax
from jax.experimental import pallas as pl
from jax.experimental.pallas import tpu as pltpu
from jax.sharding import PartitionSpec as P

HEAD_DIM = 64
ROWS = 12
SCALE = 0.125
NEG = -1e30
GROUP = 4
VMEM = pltpu.VMEM


def swap(value, bit):
    size = lax.axis_size("frame")
    return lax.ppermute(value, "frame", [(i, i ^ 1 << bit) for i in range(size)])


def from_low(value):
    size = lax.axis_size("space")
    return lax.ppermute(value, "space", [(i, i + 1) for i in range(size - 1)])


def from_high(value):
    size = lax.axis_size("space")
    return lax.ppermute(value, "space", [(i + 1, i) for i in range(size - 1)])


def pack_kernel(q, k, v, g, ko, vo, qgo, first, last):
    rows = q.shape[0]
    flat = (q.shape[1] * q.shape[2], q.shape[3])
    for row in range(rows):
        for slot, (source, target) in enumerate(
            ((k, ko.at[row]), (v, vo.at[row]), (q, qgo.at[0, row]), (g, qgo.at[1, row]))
        ):
            value = source[row].reshape(flat)
            target[...] = value
            if row == 0:
                first[slot] = value
            if row == rows - 1:
                last[slot] = value


def head_rows(value, lane_head):
    zero = jnp.zeros_like(value)
    return jnp.concatenate([jnp.where(lane_head == h, value, zero) for h in range(GROUP)], axis=0)


def head_lanes(stacked, lane_head):
    tokens = stacked.shape[0] // GROUP
    total = stacked[:tokens]
    for h in range(1, GROUP):
        total = jnp.where(lane_head == h, stacked[h * tokens : (h + 1) * tokens], total)
    return total


def nt(a, b):
    return lax.dot_general(a, b, (((1,), (1,)), ((), ())), preferred_element_type=jnp.float32)


def nn(a, b):
    return jnp.dot(a, b, preferred_element_type=jnp.float32)


def forward_kernel(count, bias, q, g, *refs):
    k_refs = refs[: 3 * count]
    v_refs = refs[3 * count : 6 * count]
    out, dq, stats = refs[6 * count :]
    rows, tokens, width = q.shape

    def piece(group, block, row):
        low, mid, high = group[3 * block : 3 * block + 3]
        if row < 0:
            return low[...]
        if row >= rows:
            return high[...]
        return mid[row]

    def window(group, row):
        return jnp.concatenate(
            [piece(group, b, row + shift) for shift in (-1, 0, 1) for b in range(count)], axis=0
        )

    lane_head = lax.broadcasted_iota(jnp.int32, (tokens, width), 1) // HEAD_DIM
    lane = lax.broadcasted_iota(jnp.int32, (GROUP * tokens, 128), 1)
    columns = jnp.zeros((GROUP * tokens, 128), jnp.float32)
    for row in range(rows):
        k_win = window(k_refs, row)
        v_win = window(v_refs, row)
        keys = k_win.shape[0]
        scores = nt(head_rows(q[row] * SCALE, lane_head), k_win)
        scores = (scores.reshape(-1, 8, keys) + bias[row][None]).reshape(scores.shape)
        top = jnp.max(scores, axis=1, keepdims=True)
        raw = jnp.exp(scores - top)
        total = jnp.sum(raw, axis=1, keepdims=True)
        probs = raw * (1.0 / total)
        attended = head_lanes(nn(probs.astype(jnp.bfloat16), v_win), lane_head)
        attended = attended.astype(jnp.bfloat16)
        out[row] = attended
        grad = g[row]
        prod = grad.astype(jnp.float32) * attended.astype(jnp.float32)
        delta = jnp.sum(head_rows(prod, lane_head), axis=1, keepdims=True)
        grad_probs = nt(head_rows(grad, lane_head), v_win)
        grad_scores = (probs * (grad_probs - delta)).astype(jnp.bfloat16)
        dq[row] = (head_lanes(nn(grad_scores, k_win), lane_head) * SCALE).astype(jnp.bfloat16)
        columns = jnp.where(lane == 2 * row, top + jnp.log(total), columns)
        columns = jnp.where(lane == 2 * row + 1, delta, columns)
    turned = columns.T
    for row in range(rows):
        for which in range(2):
            line = turned[2 * row + which : 2 * row + which + 1]
            for h in range(GROUP):
                at = which * GROUP + h
                stats[row, at : at + 1, :] = line[:, h * tokens : (h + 1) * tokens]


def backward_kernel(count, bias, k, v, *refs):
    q_refs = refs[: 3 * count]
    g_refs = refs[3 * count : 6 * count]
    s_refs = refs[6 * count : 9 * count]
    dk, dv = refs[9 * count :]
    rows, tokens, width = k.shape

    def piece(group, block, row):
        low, mid, high = group[3 * block : 3 * block + 3]
        if row < 0:
            return low[...]
        if row >= rows:
            return high[...]
        return mid[row]

    def window(group, row, axis):
        return jnp.concatenate(
            [piece(group, b, row + shift) for shift in (-1, 0, 1) for b in range(count)], axis=axis
        )

    lane_head = lax.broadcasted_iota(jnp.int32, (tokens, width), 1) // HEAD_DIM

    def spread(lines):
        return jnp.concatenate(
            [jnp.broadcast_to(lines[h : h + 1], (tokens, lines.shape[1])) for h in range(GROUP)],
            axis=0,
        )

    for row in range(rows):
        q_win = window(q_refs, row, 0)
        g_win = window(g_refs, row, 0)
        stat = window(s_refs, row, 1)
        lse = spread(stat[:GROUP] + bias[row][:GROUP])
        delta = spread(stat[GROUP:])
        scores = nt(head_rows(k[row] * SCALE, lane_head), q_win)
        probs = jnp.exp(scores - lse)
        dv[row] = head_lanes(nn(probs.astype(jnp.bfloat16), g_win), lane_head).astype(jnp.bfloat16)
        grad_probs = nt(head_rows(v[row], lane_head), g_win)
        grad_scores = (probs * (grad_probs - delta)).astype(jnp.bfloat16)
        dk[row] = (head_lanes(nn(grad_scores, q_win), lane_head) * SCALE).astype(jnp.bfloat16)


def lanes(array, width):
    shape = array.shape[:-1] + (width,)
    zeros = (0,) * (array.ndim - 1)
    return pl.BlockSpec(shape, lambda i: zeros + (i,))


def slot_lanes(array, slots, width):
    kept = array.shape[len(slots) : -1]
    shape = (None,) * len(slots) + kept + (width,)
    return pl.BlockSpec(shape, lambda i: slots + (0,) * len(kept) + (i,))


def lead(array, slots=()):
    kept = array.shape[1 + len(slots) :]
    shape = (None,) * (1 + len(slots)) + kept
    return pl.BlockSpec(shape, lambda i: (i,) + slots + (0,) * len(kept))


def whole(array):
    zeros = (0,) * array.ndim
    return pl.BlockSpec(array.shape, lambda i: zeros)


def per_device(query_vectors, key_vectors, value_vectors, out_cotangent, partner_mask):
    frames, rows, columns, width = query_vectors.shape
    bits = min(4, lax.axis_size("frame").bit_length() - 1)
    count = bits + 1
    tokens = frames * columns
    heads = width // HEAD_DIM
    groups = heads // GROUP
    part = GROUP * HEAD_DIM
    frame_index = lax.axis_index("frame")
    band = lax.axis_index("space")

    turn = lambda a: jnp.transpose(a, (1, 2, 0, 3))
    sds = lambda *shape: jax.ShapeDtypeStruct(shape, jnp.bfloat16)
    k, v, qg, first, last = pl.pallas_call(
        pack_kernel,
        out_shape=(
            sds(rows, tokens, width),
            sds(rows, tokens, width),
            sds(2, rows, tokens, width),
            sds(4, tokens, width),
            sds(4, tokens, width),
        ),
        name="pack",
    )(turn(query_vectors), turn(key_vectors), turn(value_vectors), turn(out_cotangent))

    ext = band * rows - 1 + jnp.arange(rows + 2)
    ext_ok = (ext >= 0) & (ext < ROWS)
    row_ok = jnp.stack([ext_ok[r : r + 3] for r in range(rows)])
    own_mask = lax.dynamic_slice_in_dim(partner_mask, frame_index * frames, frames, 0) == 1
    block_ok = jnp.concatenate([jnp.ones((frames, 1), bool), own_mask], axis=1)
    allowed = row_ok[:, None, :, None] & block_ok[None, :, None, :]
    bias_f = jnp.where(allowed, 0.0, NEG).astype(jnp.float32)
    bias_f = jnp.broadcast_to(bias_f[..., None], (rows, frames, 3, count, tokens))
    bias_f = bias_f.reshape(rows, 1, frames, 3 * count * tokens)
    bias_f = jnp.broadcast_to(bias_f, (rows, 8 // frames, frames, 3 * count * tokens))
    bias_f = bias_f.reshape(rows, 8, -1)
    partner_rows = [jnp.ones((frames,), bool)]
    for bit in range(bits):
        theirs = lax.dynamic_slice_in_dim(partner_mask, (frame_index ^ (1 << bit)) * frames, frames, 0)
        partner_rows.append(theirs[:, bit] == 1)
    partner_ok = jnp.stack(partner_rows)
    allowed = row_ok[:, :, None, None] & partner_ok[None, None]
    bias_b = jnp.where(allowed, 0.0, -NEG).astype(jnp.float32)
    bias_b = jnp.broadcast_to(bias_b[:, :, :, None, :], (rows, 3, count, columns, frames))
    bias_b = jnp.broadcast_to(bias_b.reshape(rows, 1, -1), (rows, 8, 3 * count * tokens))

    k_part = [swap(k, bit) for bit in range(bits)]
    v_part = [swap(v, bit) for bit in range(bits)]
    qg_part = [swap(qg, bit) for bit in range(bits)]
    own_low, own_high = from_low(last), from_high(first)
    edge = lambda parts, index: jnp.stack([p[..., index, :, :] for p in parts])
    k_low, k_high = from_low(edge(k_part, rows - 1)), from_high(edge(k_part, 0))
    v_low, v_high = from_low(edge(v_part, rows - 1)), from_high(edge(v_part, 0))
    qg_low, qg_high = from_low(edge(qg_part, rows - 1)), from_high(edge(qg_part, 0))

    args, specs = [bias_f, qg, qg], [whole(bias_f), slot_lanes(qg, (0,), part), slot_lanes(qg, (1,), part)]
    for slot, own, parts, low, high in ((0, k, k_part, k_low, k_high), (1, v, v_part, v_low, v_high)):
        args += [own_low, own, own_high]
        specs += [slot_lanes(own_low, (slot,), part), lanes(own, part), slot_lanes(own_high, (slot,), part)]
        for bit in range(bits):
            args += [low, parts[bit], high]
            specs += [slot_lanes(low, (bit,), part), lanes(parts[bit], part), slot_lanes(high, (bit,), part)]
    attended, dq, stats = pl.pallas_call(
        functools.partial(forward_kernel, count),
        grid=(groups,),
        in_specs=specs,
        out_shape=(
            sds(rows, tokens, width),
            sds(rows, tokens, width),
            jax.ShapeDtypeStruct((groups, rows, 2 * GROUP, tokens), jnp.float32),
        ),
        out_specs=(
            pl.BlockSpec((rows, tokens, part), lambda i: (0, 0, i)),
            pl.BlockSpec((rows, tokens, part), lambda i: (0, 0, i)),
            pl.BlockSpec((None, rows, 2 * GROUP, tokens), lambda i: (i, 0, 0, 0)),
        ),
        name="forward",
    )(*args)

    s_part = [swap(stats, bit) for bit in range(bits)]
    s_all = jnp.stack([stats] + s_part)
    s_low, s_high = from_low(s_all[:, :, rows - 1]), from_high(s_all[:, :, 0])

    args, specs = [bias_b, k, v], [whole(bias_b), lanes(k, part), lanes(v, part)]
    for slot in range(2):
        args += [own_low, qg, own_high]
        specs += [slot_lanes(own_low, (2 + slot,), part), slot_lanes(qg, (slot,), part), slot_lanes(own_high, (2 + slot,), part)]
        for bit in range(bits):
            args += [qg_low, qg_part[bit], qg_high]
            specs += [slot_lanes(qg_low, (bit, slot), part), slot_lanes(qg_part[bit], (slot,), part), slot_lanes(qg_high, (bit, slot), part)]
    for block in range(count):
        edge_spec = pl.BlockSpec((None, None, 2 * GROUP, tokens), lambda i, block=block: (block, i, 0, 0))
        args += [s_low, s_all, s_high]
        specs += [edge_spec, pl.BlockSpec((None, None, rows, 2 * GROUP, tokens), lambda i, block=block: (block, i, 0, 0, 0)), edge_spec]
    dk, dv = pl.pallas_call(
        functools.partial(backward_kernel, count),
        grid=(groups,),
        in_specs=specs,
        out_shape=(sds(rows, tokens, width), sds(rows, tokens, width)),
        out_specs=(
            pl.BlockSpec((rows, tokens, part), lambda i: (0, 0, i)),
            pl.BlockSpec((rows, tokens, part), lambda i: (0, 0, i)),
        ),
        name="backward",
    )(*args)
    back = lambda a: jnp.transpose(a.reshape(rows, columns, frames, width), (2, 0, 1, 3))
    return back(attended), back(dq), back(dk), back(dv)


def solution(mesh):
    spec = P("frame", "space", None, None)
    return jax.shard_map(
        per_device,
        mesh=mesh,
        in_specs=(spec, spec, spec, spec, P()),
        out_specs=(spec, spec, spec, spec),
        check_vma=False,
    )
```

```python
import functools

import jax
import jax.numpy as jnp
from jax import lax
from jax.experimental import pallas as pl
from jax.experimental.pallas import tpu as pltpu
from jax.sharding import PartitionSpec as P


HEAD_DIM = 64
SCALE = 0.125
NEG = -1e30
PAIR = 2 * HEAD_DIM
PAIRS = 2
PART = PAIRS * PAIR
CHUNK = 16
BF16 = jnp.bfloat16
F32 = jnp.float32


def swap(value, bit):
    size = lax.axis_size("frame")
    return lax.ppermute(value, "frame", [(i, i ^ 1 << bit) for i in range(size)])


def swaps(value, bits):
    return [swap(value, bit) for bit in range(bits)]


def exchange(value, side):
    pairs = []
    for low in range(side, lax.axis_size("space") - 1, 2):
        pairs += [(low, low + 1), (low + 1, low)]
    return lax.ppermute(value, "space", pairs)


def struct(*shape, dtype=BF16):
    return jax.ShapeDtypeStruct(shape, dtype)


def call(kernel, outs, ins, flops=0, exps=0, scratch=(), limit=4 << 20, table=None, to_hbm=()):
    size = sum(a.size * a.dtype.itemsize for a in ins) + sum(
        o.size * jnp.dtype(o.dtype).itemsize for o in outs
    )
    ins = [pltpu.with_memory_space_constraint(a, pltpu.VMEM) for a in ins]
    specs = [pl.BlockSpec(memory_space=pltpu.VMEM) for _ in ins]
    if table is not None:
        ins = ins + [table]
        specs = specs + [pl.BlockSpec(memory_space=pltpu.SMEM)]
    return pl.pallas_call(
        kernel,
        out_shape=tuple(
            o if i in to_hbm else pltpu.VMEM(o.shape, o.dtype) for i, o in enumerate(outs)
        ),
        in_specs=specs,
        out_specs=tuple(pl.BlockSpec(memory_space=pltpu.VMEM) for _ in outs),
        scratch_shapes=list(scratch),
        compiler_params=pltpu.CompilerParams(vmem_limit_bytes=limit),
        cost_estimate=pl.CostEstimate(flops=flops, bytes_accessed=size, transcendentals=exps),
    )(*ins)


def edge_rows(rows):
    odd = lax.rem(lax.axis_index("space"), 2)
    return (rows - 1) * (1 - odd), (rows - 1) * odd


def pack_kernel(n, *refs):
    sources, (packed, *edges) = refs[:n], refs[-3:]
    rows, columns, frames, width = sources[0].shape
    for at, source in enumerate(sources):
        for row in range(rows):
            packed[at * rows + row] = source[row].reshape(columns * frames, width)
        for edge, row in zip(edges, edge_rows(rows)):
            edge[at] = source[row].reshape(columns * frames, width)


def pack(sources, after=()):
    rows, columns, frames, width = sources[0].shape
    edge = struct(len(sources), columns * frames, width)
    outs = [struct(len(sources) * rows, columns * frames, width), edge, edge]
    kernel = functools.partial(pack_kernel, len(sources))
    return call(kernel, outs, sources + list(after))


def join_kernel(*refs):
    sources, target = refs[:-1], refs[-1]
    for at, source in enumerate(sources):
        for slot in range(source.shape[0]):
            target[at * source.shape[0] + slot] = source[slot]


def join(sources):
    shape = (len(sources) * sources[0].shape[0],) + sources[0].shape[1:]
    return call(join_kernel, [struct(*shape, dtype=sources[0].dtype)], sources)[0]


def head_rows(value, lane_head):
    zero = jnp.zeros_like(value)
    return jnp.concatenate([jnp.where(lane_head == h, value, zero) for h in range(2)], axis=0)


def head_lanes(stacked, lane_head):
    tokens = stacked.shape[0] // 2
    return jnp.where(lane_head == 0, stacked[:tokens], stacked[tokens:])


def nt(a, b):
    return lax.dot_general(a, b, (((1,), (1,)), ((), ())), preferred_element_type=F32)


def nn(a, b):
    return jnp.dot(a, b, preferred_element_type=F32)


class Pieces:
    def __init__(self, refs, rows, mids, rim_slots):
        self.rows = rows
        self.mids = [(refs[i], s) for i, s in mids]
        self.rims = [[(refs[i], s) for i, s in side] for side in rim_slots]

    def window(self, kind, lanes):
        out = []
        for at in range(3):
            for block, (mid, base) in enumerate(self.mids):
                if isinstance(kind, int):
                    out.append(mid[base + kind - 1 + at, :, lanes])
                elif at == 0:
                    ref, slot = self.rims[int(kind)][block]
                    out.append(ref[slot, :, lanes])
                else:
                    edge = edge_rows(self.rows)[int(kind)]
                    inner = jnp.where(edge == 0, 1, edge - 1)
                    out.append(mid[base + (edge if at == 1 else inner), :, lanes])
        return jnp.concatenate(out, axis=0)


def row_of(kind, rows):
    return kind if isinstance(kind, int) else edge_rows(rows)[int(kind)]


def rim_open(side):
    band, size = lax.axis_index("space"), lax.axis_size("space")
    odd = lax.rem(band, 2)
    up = (odd == 0) if side == 0 else (odd == 1)
    other = jnp.where(up, band + 1, band - 1)
    return (other >= 0) & (other < size)


def build_masks(mask_ref, kinds, blocks, frames, tokens, table, queries_here):
    shape = (8, blocks * tokens)
    lane = lax.broadcasted_iota(jnp.int32, shape, 1)
    sub = lax.broadcasted_iota(jnp.int32, shape, 0)
    bad = NEG if queries_here else -NEG
    which = sub if queries_here else lane
    which = lax.rem(which, frames)
    group = lane // tokens
    here = lax.axis_index("frame")
    value = jnp.zeros(shape, F32)
    for block in range(1, blocks):
        owner = here if queries_here else jnp.bitwise_xor(here, 1 << (block - 1))
        for frame in range(frames):
            off = jnp.where(table[block - 1, owner * frames + frame] == 1, 0.0, bad)
            value = jnp.where((group == block) & (which == frame), off.astype(F32), value)
    for slot, kind in enumerate(kinds):
        first = value
        if not isinstance(kind, int):
            first = value + jnp.where(rim_open(int(kind)), 0.0, bad).astype(F32)
        mask_ref[slot] = jnp.concatenate([first, value, value], axis=1)


def forward_kernel(layout, kinds, carried, *refs):
    qg = refs[layout["own"]]
    rows = qg.shape[0] // 2
    keys, values = (Pieces(refs, rows, *layout[name]) for name in ("k", "v"))
    n_in = layout["n_in"]
    table = refs[n_in]
    out, dq, stats = refs[n_in + 1 :][:3]
    mask, s_scr, d_scr, p_scr = refs[-4:]
    tokens, width = qg.shape[1:]
    columns, frames = out.shape[1:3]
    count = len(keys.mids)
    if carried:
        for target, source in zip((out, dq), refs[n_in - 3 : n_in - 1]):
            for at, row in enumerate(carried):
                target[row] = source[at]
        for at in range(len(carried)):
            stats[at] = refs[n_in - 1][at]
    build_masks(mask, kinds, count, frames, tokens, table, True)
    lane_head = lax.broadcasted_iota(jnp.int32, (tokens, PAIR), 1) // HEAD_DIM
    lane = lax.broadcasted_iota(jnp.int32, (2 * tokens, 128), 1)
    slot_of = lambda row: row if carried else row - 1
    units = [(slot, pair) for slot in range(len(kinds)) for pair in range(PAIRS)]

    def step(group, _):
        starts = [pl.multiple_of(group * PART + pair * PAIR, PAIR) for pair in range(PAIRS)]
        lanes_of = [pl.ds(start, PAIR) for start in starts]
        for unit, (slot, pair) in enumerate(units):
            lanes, kind = lanes_of[pair], kinds[slot]
            row = row_of(kind, rows)
            s_scr[unit] = nt(head_rows(qg[row, :, lanes] * SCALE, lane_head), keys.window(kind, lanes))
            d_scr[unit] = nt(head_rows(qg[rows + row, :, lanes], lane_head), values.window(kind, lanes))
        tops, totals = [], []
        for unit, (slot, pair) in enumerate(units):
            top_parts, total_parts = [], []
            bias = jnp.concatenate([mask[slot]] * (CHUNK // 8), axis=0)
            for start in range(0, 2 * tokens, CHUNK):
                scores = s_scr[unit, start : start + CHUNK, :] + bias
                top = jnp.max(scores, axis=1, keepdims=True)
                raw = jnp.exp(scores - top)
                s_scr[unit, start : start + CHUNK, :] = raw
                p_scr[unit, start : start + CHUNK, :] = raw.astype(BF16)
                top_parts.append(top)
                total_parts.append(jnp.sum(raw, axis=1, keepdims=True))
            tops.append(jnp.concatenate(top_parts, axis=0))
            totals.append(jnp.concatenate(total_parts, axis=0))
        cols = jnp.zeros((2 * tokens, 128), F32)
        deltas, scales = [], []
        for unit, (slot, pair) in enumerate(units):
            lanes, kind = lanes_of[pair], kinds[slot]
            row = row_of(kind, rows)
            scale = 1.0 / totals[unit]
            wide = nn(p_scr[unit], values.window(kind, lanes)) * scale
            attended = head_lanes(wide, lane_head).astype(BF16)
            out[slot_of(row), :, :, lanes] = attended.reshape(columns, frames, PAIR)
            prod = qg[rows + row, :, lanes].astype(F32) * attended.astype(F32)
            delta = jnp.sum(head_rows(prod, lane_head), axis=1, keepdims=True)
            deltas.append(delta)
            scales.append(scale)
            cols = jnp.where(lane == 2 * unit, tops[unit] + jnp.log(totals[unit]), cols)
            cols = jnp.where(lane == 2 * unit + 1, delta, cols)
        for unit, (slot, pair) in enumerate(units):
            for start in range(0, 2 * tokens, CHUNK):
                part = slice(start, start + CHUNK)
                grad_scores = s_scr[unit, part, :] * (d_scr[unit, part, :] - deltas[unit][part])
                p_scr[unit, part, :] = grad_scores.astype(BF16)
        for unit, (slot, pair) in enumerate(units):
            lanes, kind = lanes_of[pair], kinds[slot]
            wide = nn(p_scr[unit], keys.window(kind, lanes)) * (scales[unit] * SCALE)
            grad_q = head_lanes(wide, lane_head).astype(BF16)
            dq[slot_of(row_of(kind, rows)), :, :, lanes] = grad_q.reshape(columns, frames, PAIR)
        turned = cols.T
        for unit, (slot, pair) in enumerate(units):
            for which in range(2):
                line = turned[2 * unit + which : 2 * unit + which + 1]
                for h in range(2):
                    to = which * 2 * PAIRS + pair * 2 + h
                    stats[len(carried) + slot, group, to : to + 1, :] = line[:, h * tokens : (h + 1) * tokens]
        return 0

    lax.fori_loop(0, width // PART, step, 0)


def backward_kernel(layout, kinds, carried, *refs):
    kv = refs[layout["own"]]
    rows = kv.shape[0] // 2
    queries, grads = (Pieces(refs, rows, *layout[name]) for name in ("q", "g"))
    n_in = layout["n_in"]
    table = refs[n_in]
    dk, dv = refs[n_in + 1 :][:2]
    mask, s_scr, d_scr, p_scr, t_scr = refs[-5:]
    tokens, width = kv.shape[1:]
    columns, frames = dk.shape[1:3]
    count = len(queries.mids)
    for target, source in zip((dk, dv), refs[n_in - 2 : n_in]):
        for at, row in enumerate(carried):
            target[row] = source[at]
    build_masks(mask, kinds, count, frames, tokens, table, False)
    lane_head = lax.broadcasted_iota(jnp.int32, (tokens, PAIR), 1) // HEAD_DIM
    slot_of = lambda row: row if carried else row - 1
    units = [(slot, pair) for slot in range(len(kinds)) for pair in range(PAIRS)]

    def stat_window(kind, group):
        out = []
        mids, rim = layout["s"]
        inner = rows - 2

        def stat_at(block, row):
            if isinstance(row, int) and 0 < row < rows - 1:
                return refs[mids[block]][row - 1, group]
            first, _ = edge_rows(rows)
            return refs[mids[block]][jnp.where(first == row, inner, inner + 1), group]

        for at in range(3):
            for block in range(count):
                if isinstance(kind, int):
                    out.append(stat_at(block, kind - 1 + at))
                elif at == 0:
                    index, slot = rim[int(kind)][block]
                    out.append(refs[index][slot, group])
                elif at == 1:
                    out.append(refs[mids[block]][inner + int(kind), group])
                else:
                    place = edge_rows(rows)[int(kind)]
                    out.append(refs[mids[block]][jnp.where(place == 0, 1, place - 1) - 1, group])
        return jnp.concatenate(out, axis=1)

    def step(group, _):
        lanes_of = [pl.ds(pl.multiple_of(group * PART + pair * PAIR, PAIR), PAIR) for pair in range(PAIRS)]
        for unit, (slot, pair) in enumerate(units):
            lanes, kind = lanes_of[pair], kinds[slot]
            row = row_of(kind, rows)
            s_scr[unit] = nt(head_rows(kv[row, :, lanes] * SCALE, lane_head), queries.window(kind, lanes))
            d_scr[unit] = nt(head_rows(kv[rows + row, :, lanes], lane_head), grads.window(kind, lanes))
        stats = [stat_window(kind, group) for kind in kinds]
        for unit, (slot, pair) in enumerate(units):
            stat = stats[slot]
            for h in range(2):
                at = pair * 2 + h
                lse = stat[at : at + 1] + mask[slot, 0:1]
                delta = stat[2 * PAIRS + at : 2 * PAIRS + at + 1]
                for start in range(h * tokens, (h + 1) * tokens, CHUNK):
                    part = slice(start, start + CHUNK)
                    probs = jnp.exp(s_scr[unit, part, :] - lse)
                    p_scr[unit, part, :] = probs.astype(BF16)
                    t_scr[unit, part, :] = (probs * (d_scr[unit, part, :] - delta)).astype(BF16)
        for unit, (slot, pair) in enumerate(units):
            lanes, kind = lanes_of[pair], kinds[slot]
            row = row_of(kind, rows)
            grad_v = head_lanes(nn(p_scr[unit], grads.window(kind, lanes)), lane_head).astype(BF16)
            dv[slot_of(row), :, :, lanes] = grad_v.reshape(columns, frames, PAIR)
            grad_k = head_lanes(nn(t_scr[unit], queries.window(kind, lanes)), lane_head) * SCALE
            dk[slot_of(row), :, :, lanes] = grad_k.astype(BF16).reshape(columns, frames, PAIR)
        return 0

    lax.fori_loop(0, width // PART, step, 0)


def per_device(query_vectors, key_vectors, value_vectors, out_cotangent, partner_mask):
    frames, rows, columns, width = query_vectors.shape
    bits = min(4, lax.axis_size("frame").bit_length() - 1)
    count = bits + 1
    tokens = frames * columns
    groups = width // PART
    window = 3 * count * tokens
    table = partner_mask.T
    turn = lambda a: jnp.transpose(a, (1, 2, 0, 3))
    back = lambda a: jnp.transpose(a, (2, 0, 1, 3))

    kv, kv_edge0, kv_edge1 = pack([turn(key_vectors), turn(value_vectors)])
    kvs = [kv] + swaps(kv, bits)
    kv_rims = [exchange(kv_edge0, 0), exchange(kv_edge1, 1)]
    kv_rims_of = swaps(join(kv_rims), bits)
    qg, qg_edge0, qg_edge1 = pack([turn(query_vectors), turn(out_cotangent)], [kv_edge0])
    qg_rims = [exchange(qg_edge0, 0), exchange(qg_edge1, 1)]
    qgs = [qg] + swaps(qg, bits)
    qg_rims_of = swaps(join(qg_rims), bits)

    inner_kinds = list(range(1, rows - 1))
    edge_kinds = ["0", "1"]
    inner = len(inner_kinds)
    work = 4 * 2 * (width // PAIR) * 2 * tokens * window * PAIR
    exps = (width // HEAD_DIM) * tokens * window
    line = lambda n: struct(n, columns, frames, width)

    def scratches(n, extra):
        units = n * PAIRS
        wide = [pltpu.VMEM((n, 8, window), F32)]
        wide += [pltpu.VMEM((units, 2 * tokens, window), F32)] * 2
        return wide + [pltpu.VMEM((units, 2 * tokens, window), BF16)] * extra

    def gathered(at, rim_at, tensor):
        mids = [(at + block, tensor * rows) for block in range(count)]
        if rim_at is None:
            return mids, []
        sides = []
        for side in range(2):
            own = [(rim_at + side, tensor)]
            sides.append(own + [(rim_at + 2 + bit, 2 * side + tensor) for bit in range(bits)])
        return mids, sides

    stat = lambda n: struct(n, groups, 4 * PAIRS, tokens, dtype=F32)
    ins = [qg] + kvs
    layout = {"n_in": len(ins), "own": 0, "k": gathered(1, None, 0), "v": gathered(1, None, 1)}
    inner_out = call(
        functools.partial(forward_kernel, layout, inner_kinds, ()),
        [line(inner), line(inner), stat(inner)], ins,
        flops=work * inner, exps=exps * inner, scratch=scratches(inner, 1), limit=10 << 20, table=table,
    )
    rim_at = len(ins)
    ins = ins + kv_rims + kv_rims_of + list(inner_out)
    layout = {"n_in": len(ins), "own": 0, "k": gathered(1, rim_at, 0), "v": gathered(1, rim_at, 1)}
    attended, dq, stats = call(
        functools.partial(forward_kernel, layout, edge_kinds, inner_kinds),
        [line(rows), line(rows), stat(rows)], ins, to_hbm=(0, 1),
        flops=work * 2, exps=exps * 2, scratch=scratches(2, 1), limit=10 << 20, table=table,
    )
    ss = [stats] + swaps(stats, bits)

    def stat_edge_kernel(*refs):
        for slot, source in enumerate(refs[:-2]):
            for side in range(2):
                refs[len(refs) - 2 + side][slot] = source[inner + side]

    s_rims = call(stat_edge_kernel, [stat(count)] * 2, ss)
    s_rims = [exchange(edge, side) for side, edge in enumerate(s_rims)]

    ins = [kv] + qgs + ss
    mids = range(1 + count, 1 + 2 * count)
    layout = {"n_in": len(ins), "own": 0, "q": gathered(1, None, 0), "g": gathered(1, None, 1), "s": (mids, None)}
    inner_out = call(
        functools.partial(backward_kernel, layout, inner_kinds, ()),
        [line(inner), line(inner)], ins,
        flops=work * inner, exps=exps * inner, scratch=scratches(inner, 2), limit=10 << 20, table=table,
    )
    rim_at = len(ins)
    ins = ins + qg_rims + qg_rims_of + s_rims + list(inner_out)
    rim = [[(rim_at + 2 + bits + side, block) for block in range(count)] for side in range(2)]
    layout = {"n_in": len(ins), "own": 0, "q": gathered(1, rim_at, 0), "g": gathered(1, rim_at, 1), "s": (mids, rim)}
    dk, dv = call(
        functools.partial(backward_kernel, layout, edge_kinds, inner_kinds),
        [line(rows), line(rows)], ins, to_hbm=(0, 1),
        flops=work * 2, exps=exps * 2, scratch=scratches(2, 2), limit=10 << 20, table=table,
    )
    return back(attended), back(dq), back(dk), back(dv)


def solution(mesh):
    spec = P("frame", "space", None, None)

    return jax.shard_map(
        per_device,
        mesh=mesh,
        in_specs=(spec, spec, spec, spec, P()),
        out_specs=(spec, spec, spec, spec),
        check_vma=False,
    )
```

```python
import functools

import jax
import jax.numpy as jnp
from jax import lax
from jax.experimental import pallas as pl
from jax.experimental.pallas import tpu as pltpu
from jax.sharding import PartitionSpec as P


HEAD_DIM = 64
SCALE = 0.125
NEG = -1e30
PAIR = 2 * HEAD_DIM
PAIRS = 2
PART = PAIRS * PAIR
CHUNK = 16
BF16 = jnp.bfloat16
F32 = jnp.float32


def swap(value, bit):
    size = lax.axis_size("frame")
    return lax.ppermute(value, "frame", [(i, i ^ 1 << bit) for i in range(size)])


def swaps(value, bits):
    return [swap(value, bit) for bit in range(bits)]


def exchange(value, side):
    pairs = []
    for low in range(side, lax.axis_size("space") - 1, 2):
        pairs += [(low, low + 1), (low + 1, low)]
    return lax.ppermute(value, "space", pairs)


def struct(*shape, dtype=BF16):
    return jax.ShapeDtypeStruct(shape, dtype)


def call(kernel, outs, ins, flops=0, exps=0, scratch=(), limit=4 << 20, table=None, to_hbm=()):
    size = sum(a.size * a.dtype.itemsize for a in ins) + sum(
        o.size * jnp.dtype(o.dtype).itemsize for o in outs
    )
    ins = [pltpu.with_memory_space_constraint(a, pltpu.VMEM) for a in ins]
    specs = [pl.BlockSpec(memory_space=pltpu.VMEM) for _ in ins]
    if table is not None:
        ins = ins + [table]
        specs = specs + [pl.BlockSpec(memory_space=pltpu.SMEM)]
    return pl.pallas_call(
        kernel,
        out_shape=tuple(
            o if i in to_hbm else pltpu.VMEM(o.shape, o.dtype) for i, o in enumerate(outs)
        ),
        in_specs=specs,
        out_specs=tuple(pl.BlockSpec(memory_space=pltpu.VMEM) for _ in outs),
        scratch_shapes=list(scratch),
        compiler_params=pltpu.CompilerParams(vmem_limit_bytes=limit),
        cost_estimate=pl.CostEstimate(flops=flops, bytes_accessed=size, transcendentals=exps),
    )(*ins)


def edge_rows(rows):
    odd = lax.rem(lax.axis_index("space"), 2)
    return (rows - 1) * (1 - odd), (rows - 1) * odd


def pack_kernel(n, *refs):
    sources, (packed, *edges) = refs[:n], refs[-3:]
    rows, columns, frames, width = sources[0].shape
    for at, source in enumerate(sources):
        for row in range(rows):
            packed[at * rows + row] = source[row].reshape(columns * frames, width)
        for edge, row in zip(edges, edge_rows(rows)):
            edge[at] = source[row].reshape(columns * frames, width)


def pack(sources, after=()):
    rows, columns, frames, width = sources[0].shape
    edge = struct(len(sources), columns * frames, width)
    outs = [struct(len(sources) * rows, columns * frames, width), edge, edge]
    kernel = functools.partial(pack_kernel, len(sources))
    return call(kernel, outs, sources + list(after))


def join_kernel(*refs):
    sources, target = refs[:-1], refs[-1]
    for at, source in enumerate(sources):
        for slot in range(source.shape[0]):
            target[at * source.shape[0] + slot] = source[slot]


def join(sources):
    shape = (len(sources) * sources[0].shape[0],) + sources[0].shape[1:]
    return call(join_kernel, [struct(*shape, dtype=sources[0].dtype)], sources)[0]


def head_rows(value, lane_head):
    zero = jnp.zeros_like(value)
    return jnp.concatenate([jnp.where(lane_head == h, value, zero) for h in range(2)], axis=0)


def head_lanes(stacked, lane_head):
    tokens = stacked.shape[0] // 2
    return jnp.where(lane_head == 0, stacked[:tokens], stacked[tokens:])


def nt(a, b):
    return lax.dot_general(a, b, (((1,), (1,)), ((), ())), preferred_element_type=F32)


def nn(a, b):
    return jnp.dot(a, b, preferred_element_type=F32)


class Pieces:
    def __init__(self, refs, rows, mids, rim_slots):
        self.rows = rows
        self.mids = [(refs[i], s) for i, s in mids]
        self.rims = [[(refs[i], s) for i, s in side] for side in rim_slots]

    def window(self, kind, lanes):
        out = []
        for at in range(3):
            for block, (mid, base) in enumerate(self.mids):
                if isinstance(kind, int):
                    out.append(mid[base + kind - 1 + at, :, lanes])
                elif at == 0:
                    ref, slot = self.rims[int(kind)][block]
                    out.append(ref[slot, :, lanes])
                else:
                    edge = edge_rows(self.rows)[int(kind)]
                    inner = jnp.where(edge == 0, 1, edge - 1)
                    out.append(mid[base + (edge if at == 1 else inner), :, lanes])
        return jnp.concatenate(out, axis=0)


def row_of(kind, rows):
    return kind if isinstance(kind, int) else edge_rows(rows)[int(kind)]


def rim_open(side):
    band, size = lax.axis_index("space"), lax.axis_size("space")
    odd = lax.rem(band, 2)
    up = (odd == 0) if side == 0 else (odd == 1)
    other = jnp.where(up, band + 1, band - 1)
    return (other >= 0) & (other < size)


def build_masks(mask_ref, blocks, frames, tokens, table, queries_here):
    shape = (8, blocks * tokens)
    lane = lax.broadcasted_iota(jnp.int32, shape, 1)
    sub = lax.broadcasted_iota(jnp.int32, shape, 0)
    bad = NEG if queries_here else -NEG
    which = sub if queries_here else lane
    which = lax.rem(which, frames)
    group = lane // tokens
    here = lax.axis_index("frame")
    value = jnp.zeros(shape, F32)
    for block in range(1, blocks):
        owner = here if queries_here else jnp.bitwise_xor(here, 1 << (block - 1))
        for frame in range(frames):
            off = jnp.where(table[block - 1, owner * frames + frame] == 1, 0.0, bad)
            value = jnp.where((group == block) & (which == frame), off.astype(F32), value)
    mask_ref[0] = value
    if queries_here:
        for side in range(2):
            mask_ref[1 + side] = value + jnp.where(rim_open(side), 0.0, bad).astype(F32)


def forward_kernel(layout, kinds, carried, *refs):
    qg = refs[layout["own"]]
    rows = qg.shape[0] // 2
    keys, values = (Pieces(refs, rows, *layout[name]) for name in ("k", "v"))
    n_in = layout["n_in"]
    table = refs[n_in]
    out, dq, stats = refs[n_in + 1 :][:3]
    mask, s_scr, d_scr, p_scr = refs[-4:]
    tokens, width = qg.shape[1:]
    columns, frames = out.shape[1:3]
    count = len(keys.mids)
    if carried:
        for target, source in zip((out, dq), refs[n_in - 3 : n_in - 1]):
            for at, row in enumerate(carried):
                target[row] = source[at]
        for at in range(len(carried)):
            stats[at] = refs[n_in - 1][at]
    build_masks(mask, count, frames, tokens, table, True)
    lane_head = lax.broadcasted_iota(jnp.int32, (tokens, PAIR), 1) // HEAD_DIM
    lane = lax.broadcasted_iota(jnp.int32, (2 * tokens, 128), 1)
    slot_of = lambda row: row if carried else row - 1
    units = [(slot, pair) for slot in range(len(kinds)) for pair in range(PAIRS)]

    def step(group, _):
        starts = [pl.multiple_of(group * PART + pair * PAIR, PAIR) for pair in range(PAIRS)]
        lanes_of = [pl.ds(start, PAIR) for start in starts]
        for unit, (slot, pair) in enumerate(units):
            lanes, kind = lanes_of[pair], kinds[slot]
            row = row_of(kind, rows)
            s_scr[unit] = nt(head_rows(qg[row, :, lanes] * SCALE, lane_head), keys.window(kind, lanes))
            d_scr[unit] = nt(head_rows(qg[rows + row, :, lanes], lane_head), values.window(kind, lanes))
        tops, totals = [], []
        for unit, (slot, pair) in enumerate(units):
            top_parts, total_parts = [], []
            first = mask[0] if isinstance(kinds[slot], int) else mask[1 + int(kinds[slot])]
            bias = jnp.concatenate([first, mask[0], mask[0]], axis=1)
            bias = jnp.concatenate([bias] * (CHUNK // 8), axis=0)
            for start in range(0, 2 * tokens, CHUNK):
                scores = s_scr[unit, start : start + CHUNK, :] + bias
                top = jnp.max(scores, axis=1, keepdims=True)
                raw = jnp.exp(scores - top)
                s_scr[unit, start : start + CHUNK, :] = raw
                p_scr[unit, start : start + CHUNK, :] = raw.astype(BF16)
                top_parts.append(top)
                total_parts.append(jnp.sum(raw, axis=1, keepdims=True))
            tops.append(jnp.concatenate(top_parts, axis=0))
            totals.append(jnp.concatenate(total_parts, axis=0))
        cols = jnp.zeros((2 * tokens, 128), F32)
        deltas, scales = [], []
        for unit, (slot, pair) in enumerate(units):
            lanes, kind = lanes_of[pair], kinds[slot]
            row = row_of(kind, rows)
            scale = 1.0 / totals[unit]
            wide = nn(p_scr[unit], values.window(kind, lanes)) * scale
            attended = head_lanes(wide, lane_head).astype(BF16)
            out[slot_of(row), :, :, lanes] = attended.reshape(columns, frames, PAIR)
            prod = qg[rows + row, :, lanes].astype(F32) * attended.astype(F32)
            delta = jnp.sum(head_rows(prod, lane_head), axis=1, keepdims=True)
            deltas.append(delta)
            scales.append(scale)
            cols = jnp.where(lane == 2 * unit, tops[unit] + jnp.log(totals[unit]), cols)
            cols = jnp.where(lane == 2 * unit + 1, delta, cols)
        for unit, (slot, pair) in enumerate(units):
            for start in range(0, 2 * tokens, CHUNK):
                part = slice(start, start + CHUNK)
                grad_scores = s_scr[unit, part, :] * (d_scr[unit, part, :] - deltas[unit][part])
                p_scr[unit, part, :] = grad_scores.astype(BF16)
        for unit, (slot, pair) in enumerate(units):
            lanes, kind = lanes_of[pair], kinds[slot]
            wide = nn(p_scr[unit], keys.window(kind, lanes)) * (scales[unit] * SCALE)
            grad_q = head_lanes(wide, lane_head).astype(BF16)
            dq[slot_of(row_of(kind, rows)), :, :, lanes] = grad_q.reshape(columns, frames, PAIR)
        turned = cols.T
        for unit, (slot, pair) in enumerate(units):
            for which in range(2):
                line = turned[2 * unit + which : 2 * unit + which + 1]
                for h in range(2):
                    to = which * 2 * PAIRS + pair * 2 + h
                    stats[len(carried) + slot, group, to : to + 1, :] = line[:, h * tokens : (h + 1) * tokens]
        return 0

    lax.fori_loop(0, width // PART, step, 0)


def backward_kernel(layout, kinds, *refs):
    n_in, count = layout["n_in"], layout["count"]
    kv = refs[0]
    qgs, stats_of = refs[1 : 1 + count], refs[1 + count : 1 + 2 * count]
    rims = refs[1 + 2 * count : n_in]
    table, *outs = refs[n_in:-5]
    mask, s_scr, d_scr, p_scr, t_scr = refs[-5:]
    rows = kv.shape[0] // 2
    tokens, width = kv.shape[1:]
    part = count * tokens
    build_masks(mask, count, layout["frames"], tokens, table, False)
    lane_head = lax.broadcasted_iota(jnp.int32, (tokens, PAIR), 1) // HEAD_DIM
    units = [(kind, pair) for kind in kinds for pair in range(PAIRS)]

    def query_rows(kind):
        inner = rows - 2
        if isinstance(kind, int):
            first, _ = edge_rows(rows)
            out = []
            for row in (kind - 1, kind, kind + 1):
                if 0 < row < rows - 1:
                    out.append((row, row - 1))
                else:
                    out.append((row, jnp.where(first == row, inner, inner + 1)))
            return out
        side = int(kind[-1])
        edge = edge_rows(rows)[side]
        if kind[0] == "r":
            return [(edge, inner + side)]
        near = jnp.where(edge == 0, 1, edge - 1)
        return [(edge, inner + side), (near, near - 1)]

    def key_rows(kind, tensor, lanes):
        if isinstance(kind, int):
            return kv[tensor * rows + kind, :, lanes]
        side = int(kind[-1])
        if kind[0] == "r":
            return rims[side][tensor, :, lanes]
        return kv[tensor * rows + edge_rows(rows)[side], :, lanes]

    def window(kind, tensor, lanes):
        found = [qg[tensor * rows + row, :, lanes] for row, _ in query_rows(kind) for qg in qgs]
        return jnp.concatenate(found, axis=0)

    def step(group, _):
        lanes_of = [pl.ds(pl.multiple_of(group * PART + pair * PAIR, PAIR), PAIR) for pair in range(PAIRS)]
        for unit, (kind, pair) in enumerate(units):
            lanes = lanes_of[pair]
            size = len(query_rows(kind)) * part
            s_scr[unit, :, :size] = nt(
                head_rows(key_rows(kind, 0, lanes) * SCALE, lane_head), window(kind, 0, lanes)
            )
            d_scr[unit, :, :size] = nt(
                head_rows(key_rows(kind, 1, lanes), lane_head), window(kind, 1, lanes)
            )
        stats = {
            kind: jnp.concatenate(
                [ref[slot, group] for _, slot in query_rows(kind) for ref in stats_of], axis=1
            )
            for kind in kinds
        }
        for unit, (kind, pair) in enumerate(units):
            stat = stats[kind]
            size = stat.shape[1]
            bias = jnp.concatenate([mask[0, 0:1]] * (size // part), axis=1)
            for h in range(2):
                at = pair * 2 + h
                lse = stat[at : at + 1] + bias
                delta = stat[2 * PAIRS + at : 2 * PAIRS + at + 1]
                for start in range(h * tokens, (h + 1) * tokens, CHUNK):
                    rows_at = slice(start, start + CHUNK)
                    probs = jnp.exp(s_scr[unit, rows_at, :size] - lse)
                    p_scr[unit, rows_at, :size] = probs.astype(BF16)
                    grad_scores = probs * (d_scr[unit, rows_at, :size] - delta)
                    t_scr[unit, rows_at, :size] = grad_scores.astype(BF16)
        for unit, (kind, pair) in enumerate(units):
            lanes = lanes_of[pair]
            size = len(query_rows(kind)) * part
            grad_v = head_lanes(nn(p_scr[unit, :, :size], window(kind, 1, lanes)), lane_head)
            grad_k = head_lanes(nn(t_scr[unit, :, :size], window(kind, 0, lanes)), lane_head) * SCALE
            for tensor, value in enumerate((grad_k, grad_v)):
                if isinstance(kind, str) and kind[0] == "r":
                    outs[int(kind[-1])][tensor, :, lanes] = value.astype(BF16)
                else:
                    row = row_of(kind, rows)
                    outs[0][tensor * rows + row, :, lanes] = value
        return 0

    lax.fori_loop(0, width // PART, step, 0)


def finish_kernel(total, part0, part1, dk, dv):
    rows, columns, frames, width = dk.shape
    for tensor, out in enumerate((dk, dv)):
        for row in range(1, rows - 1):
            out[row] = total[tensor * rows + row].astype(BF16).reshape(columns, frames, width)
        for part, row in zip((part0, part1), edge_rows(rows)):
            value = total[tensor * rows + row] + part[tensor].astype(F32)
            out[row] = value.astype(BF16).reshape(columns, frames, width)


def per_device(query_vectors, key_vectors, value_vectors, out_cotangent, partner_mask):
    frames, rows, columns, width = query_vectors.shape
    bits = min(4, lax.axis_size("frame").bit_length() - 1)
    count = bits + 1
    tokens = frames * columns
    groups = width // PART
    window = 3 * count * tokens
    table = partner_mask.T
    turn = lambda a: jnp.transpose(a, (1, 2, 0, 3))
    back = lambda a: jnp.transpose(a, (2, 0, 1, 3))

    kv, kv_edge0, kv_edge1 = pack([turn(key_vectors), turn(value_vectors)])
    kvs = [kv] + swaps(kv, bits)
    kv_rims = [exchange(kv_edge0, 0), exchange(kv_edge1, 1)]
    kv_rims_of = swaps(join(kv_rims), bits)
    qg, _, _ = pack([turn(query_vectors), turn(out_cotangent)], [kv_edge0])
    qgs = [qg] + swaps(qg, bits)

    inner_kinds = list(range(1, rows - 1))
    edge_kinds = ["0", "1"]
    inner = len(inner_kinds)
    work = 4 * 2 * (width // PAIR) * 2 * tokens * window * PAIR
    exps = (width // HEAD_DIM) * tokens * window
    line = lambda n: struct(n, columns, frames, width)

    def scratches(n, extra):
        units = n * PAIRS
        wide = [pltpu.VMEM((3, 8, count * tokens), F32)]
        wide += [pltpu.VMEM((units, 2 * tokens, window), F32)] * 2
        return wide + [pltpu.VMEM((units, 2 * tokens, window), BF16)] * extra

    def gathered(at, rim_at, tensor):
        mids = [(at + block, tensor * rows) for block in range(count)]
        if rim_at is None:
            return mids, []
        sides = []
        for side in range(2):
            own = [(rim_at + side, tensor)]
            sides.append(own + [(rim_at + 2 + bit, 2 * side + tensor) for bit in range(bits)])
        return mids, sides

    stat = lambda n: struct(n, groups, 4 * PAIRS, tokens, dtype=F32)
    ins = [qg] + kvs
    layout = {"n_in": len(ins), "own": 0, "k": gathered(1, None, 0), "v": gathered(1, None, 1)}
    inner_out = call(
        functools.partial(forward_kernel, layout, inner_kinds, ()),
        [line(inner), line(inner), stat(inner)], ins,
        flops=work * inner, exps=exps * inner, scratch=scratches(inner, 1), limit=10 << 20, table=table,
    )
    rim_at = len(ins)
    ins = ins + kv_rims + kv_rims_of + list(inner_out)
    layout = {"n_in": len(ins), "own": 0, "k": gathered(1, rim_at, 0), "v": gathered(1, rim_at, 1)}
    attended, dq, stats = call(
        functools.partial(forward_kernel, layout, edge_kinds, inner_kinds),
        [line(rows), line(rows), stat(rows)], ins, to_hbm=(0, 1),
        flops=work * 2, exps=exps * 2, scratch=scratches(2, 1), limit=10 << 20, table=table,
    )
    ss = [stats] + swaps(stats, bits)

    ins = [kv] + qgs + ss + kv_rims
    layout = {"n_in": len(ins), "count": count, "frames": frames}
    edge = struct(2, tokens, width)
    parts = call(
        functools.partial(backward_kernel, layout, ["r0", "r1"]),
        [edge, edge], ins,
        flops=work, exps=exps, scratch=scratches(2, 2), limit=10 << 20, table=table,
    )
    parts = [exchange(value, side) for side, value in enumerate(parts)]
    (total,) = call(
        functools.partial(backward_kernel, layout, inner_kinds + edge_kinds),
        [struct(2 * rows, tokens, width, dtype=F32)], ins,
        flops=2 * work, exps=2 * exps, scratch=scratches(rows, 2), limit=12 << 20, table=table,
    )
    full = struct(rows, columns, frames, width)
    dk, dv = call(finish_kernel, [full, full], [total] + parts, to_hbm=(0, 1))
    return back(attended), back(dq), back(dk), back(dv)


def solution(mesh):
    spec = P("frame", "space", None, None)

    return jax.shard_map(
        per_device,
        mesh=mesh,
        in_specs=(spec, spec, spec, spec, P()),
        out_specs=(spec, spec, spec, spec),
        check_vma=False,
    )
```

```python
import functools

import jax
import jax.numpy as jnp
from jax import lax
from jax.experimental import pallas as pl
from jax.experimental.pallas import tpu as pltpu
from jax.sharding import PartitionSpec as P


HEAD_DIM = 64
SCALE = 0.125
NEG = -1e30
PAIR = 2 * HEAD_DIM
PAIRS = 2
PART = PAIRS * PAIR
CHUNK = 16
RING = 4
BF16 = jnp.bfloat16
F32 = jnp.float32


def swap(value, bit):
    size = lax.axis_size("frame")
    return lax.ppermute(value, "frame", [(i, i ^ 1 << bit) for i in range(size)])


def swaps(value, bits):
    return [swap(value, bit) for bit in range(bits)]


def exchange(value, side):
    pairs = []
    for low in range(side, lax.axis_size("space") - 1, 2):
        pairs += [(low, low + 1), (low + 1, low)]
    return lax.ppermute(value, "space", pairs)


def struct(*shape, dtype=BF16):
    return jax.ShapeDtypeStruct(shape, dtype)


def call(kernel, outs, ins, flops=0, exps=0, scratch=(), limit=4 << 20, table=None, to_hbm=(), raw=0):
    size = sum(a.size * a.dtype.itemsize for a in ins) + sum(
        o.size * jnp.dtype(o.dtype).itemsize for o in outs
    )
    ins = [pltpu.with_memory_space_constraint(a, pltpu.HBM) for a in ins[:raw]] + [pltpu.with_memory_space_constraint(a, pltpu.VMEM) for a in ins[raw:]]
    specs = [pl.BlockSpec(memory_space=pltpu.HBM if i < raw else pltpu.VMEM) for i in range(len(ins))]
    if table is not None:
        ins = ins + [table]
        specs = specs + [pl.BlockSpec(memory_space=pltpu.SMEM)]
    return pl.pallas_call(
        kernel,
        out_shape=tuple(
            o if i in to_hbm else pltpu.VMEM(o.shape, o.dtype) for i, o in enumerate(outs)
        ),
        in_specs=specs,
        out_specs=tuple(
            pl.BlockSpec(memory_space=pl.ANY if i in to_hbm else pltpu.VMEM) for i in range(len(outs))
        ),
        scratch_shapes=list(scratch),
        compiler_params=pltpu.CompilerParams(vmem_limit_bytes=limit),
        cost_estimate=pl.CostEstimate(flops=flops, bytes_accessed=size, transcendentals=exps),
    )(*ins)


def edge_rows(rows):
    odd = lax.rem(lax.axis_index("space"), 2)
    return (rows - 1) * (1 - odd), (rows - 1) * odd


def pack_kernel(n, *refs):
    sources, (packed, edge0, edge1, *held, sems) = refs[:n], refs[-4 - n :]
    rows, columns, frames, width = sources[0].shape
    flat = (columns * frames, width)
    copies = [
        [pltpu.make_async_copy(source.at[row], held[at].at[row], sems.at[at, row]) for row in range(rows)]
        for at, source in enumerate(sources)
    ]
    for copy in sum(copies, []):
        copy.start()
    for at in range(n):
        for row in range(rows):
            copies[at][row].wait()
            packed[at * rows + row] = held[at][row].reshape(flat)
    for edge, row in zip((edge0, edge1), edge_rows(rows)):
        for at in range(n):
            edge[at] = packed[at * rows + row]


def pack(sources, after=()):
    n = len(sources)
    rows, columns, frames, width = sources[0].shape
    edge = struct(n, columns * frames, width)
    outs = [struct(n * rows, columns * frames, width), edge, edge]
    kernel = functools.partial(pack_kernel, n)
    held = [pltpu.VMEM(s.shape, s.dtype) for s in sources]
    scratch = held + [pltpu.SemaphoreType.DMA((n, rows))]
    return call(kernel, outs, sources + list(after), scratch=scratch, raw=n)


def join_kernel(side0, side1, after, both, keys):
    for side, source in enumerate((side0, side1)):
        both[2 * side] = source[0]
        both[2 * side + 1] = source[1]
        keys[side] = source[0]


def join(sources, after):
    shape = sources[0].shape[1:]
    return call(join_kernel, [struct(4, *shape), struct(2, *shape)], sources + after)


def edge_kernel(*refs):
    sources, targets = refs[:-2], refs[-2:]
    rows = sources[0].shape[0] // 2
    for slot, source in enumerate(sources):
        for target, row in zip(targets, edge_rows(rows)):
            target[slot] = source[rows + row]


def value_edges(sources):
    edge = struct(len(sources), *sources[0].shape[1:])
    return call(edge_kernel, [edge, edge], sources)


def lanes_at(group, pair):
    start = group * PART + pair * PAIR
    return slice(start, start + PAIR)


def head_rows(value, lane_head):
    zero = jnp.zeros_like(value)
    return jnp.concatenate([jnp.where(lane_head == h, value, zero) for h in range(2)], axis=0)


def head_lanes(stacked, lane_head):
    tokens = stacked.shape[0] // 2
    return jnp.where(lane_head == 0, stacked[:tokens], stacked[tokens:])


def nt(a, b):
    return lax.dot_general(a, b, (((1,), (1,)), ((), ())), preferred_element_type=F32)


def nn(a, b):
    return jnp.dot(a, b, preferred_element_type=F32)


class Pieces:
    def __init__(self, refs, rows, mids, rim_slots):
        self.rows = rows
        self.mids = [(refs[i], s) for i, s in mids]
        self.rims = [[(refs[i], s) for i, s in side] for side in rim_slots]

    def window(self, kind, lanes):
        out = []
        for at in range(3):
            for block, (mid, base) in enumerate(self.mids):
                if isinstance(kind, int):
                    out.append(mid[base + kind - 1 + at, :, lanes])
                elif at == 0:
                    ref, slot = self.rims[int(kind)][block]
                    out.append(ref[slot, :, lanes])
                else:
                    edge = edge_rows(self.rows)[int(kind)]
                    inner = jnp.where(edge == 0, 1, edge - 1)
                    out.append(mid[base + (edge if at == 1 else inner), :, lanes])
        return jnp.concatenate(out, axis=0)


def row_of(kind, rows):
    return kind if isinstance(kind, int) else edge_rows(rows)[int(kind)]


def rim_open(side):
    band, size = lax.axis_index("space"), lax.axis_size("space")
    odd = lax.rem(band, 2)
    up = (odd == 0) if side == 0 else (odd == 1)
    other = jnp.where(up, band + 1, band - 1)
    return (other >= 0) & (other < size)


def build_masks(mask_ref, blocks, frames, table, queries_here):
    shape = mask_ref.shape[1:]
    tokens = shape[1] // blocks
    lane = lax.broadcasted_iota(jnp.int32, shape, 1)
    sub = lax.broadcasted_iota(jnp.int32, shape, 0)
    bad = NEG if queries_here else -NEG
    which = sub if queries_here else lane
    which = lax.rem(which, frames)
    group = lane // tokens
    here = lax.axis_index("frame")
    value = jnp.zeros(shape, F32)
    for block in range(1, blocks):
        owner = here if queries_here else jnp.bitwise_xor(here, 1 << (block - 1))
        for frame in range(frames):
            off = jnp.where(table[block - 1, owner * frames + frame] == 1, 0.0, bad)
            value = jnp.where((group == block) & (which == frame), off.astype(F32), value)
    mask_ref[0] = value
    if queries_here:
        for side in range(2):
            mask_ref[1 + side] = value + jnp.where(rim_open(side), 0.0, bad).astype(F32)


def mask_kernel(blocks, frames, after, table, mask_f, mask_b):
    build_masks(mask_f, blocks, frames, table, True)
    build_masks(mask_b, blocks, frames, table, False)


def forward_kernel(layout, kinds, carried, *refs):
    qg = refs[layout["own"]]
    rows = qg.shape[0] // 2
    keys, values = (Pieces(refs, rows, *layout[name]) for name in ("k", "v"))
    n_in = layout["n_in"]
    mask = refs[n_in]
    out, dq, stats = refs[n_in + 1 :][:3]
    s_scr, d_scr, p_scr, _ = refs[-4:]
    tokens, width = qg.shape[1:]
    columns, frames = out.shape[1:3]
    if carried:
        for target, source in zip((out, dq), refs[n_in - 3 : n_in - 1]):
            for at, row in enumerate(carried):
                target[row] = source[at]
        for at in range(len(carried)):
            stats[at] = refs[n_in - 1][at]
    lane_head = lax.broadcasted_iota(jnp.int32, (tokens, PAIR), 1) // HEAD_DIM
    lane = lax.broadcasted_iota(jnp.int32, (2 * tokens, 128), 1)
    slot_of = lambda row: row if carried else row - 1
    units = [(slot, pair) for slot in range(len(kinds)) for pair in range(PAIRS)]

    def step(group, _):
        starts = [pl.multiple_of(group * PART + pair * PAIR, PAIR) for pair in range(PAIRS)]
        lanes_of = [pl.ds(start, PAIR) for start in starts]
        for unit, (slot, pair) in enumerate(units):
            lanes, kind = lanes_of[pair], kinds[slot]
            row = row_of(kind, rows)
            s_scr[unit] = nt(head_rows(qg[row, :, lanes] * SCALE, lane_head), keys.window(kind, lanes))
            d_scr[unit] = nt(head_rows(qg[rows + row, :, lanes], lane_head), values.window(kind, lanes))
        tops, totals = [], []
        for unit, (slot, pair) in enumerate(units):
            top_parts, total_parts = [], []
            first = mask[0] if isinstance(kinds[slot], int) else mask[1 + int(kinds[slot])]
            bias = jnp.concatenate([first, mask[0], mask[0]], axis=1)
            bias = jnp.concatenate([bias] * (CHUNK // 8), axis=0)
            for start in range(0, 2 * tokens, CHUNK):
                scores = s_scr[unit, start : start + CHUNK, :] + bias
                top = jnp.max(scores, axis=1, keepdims=True)
                raw = jnp.exp(scores - top)
                s_scr[unit, start : start + CHUNK, :] = raw
                p_scr[unit, start : start + CHUNK, :] = raw.astype(BF16)
                top_parts.append(top)
                total_parts.append(jnp.sum(raw, axis=1, keepdims=True))
            tops.append(jnp.concatenate(top_parts, axis=0))
            totals.append(jnp.concatenate(total_parts, axis=0))
        cols = jnp.zeros((2 * tokens, 128), F32)
        deltas, scales = [], []
        for unit, (slot, pair) in enumerate(units):
            lanes, kind = lanes_of[pair], kinds[slot]
            row = row_of(kind, rows)
            scale = 1.0 / totals[unit]
            wide = nn(p_scr[unit], values.window(kind, lanes)) * scale
            attended = head_lanes(wide, lane_head).astype(BF16)
            out[slot_of(row), :, :, lanes] = attended.reshape(columns, frames, PAIR)
            prod = qg[rows + row, :, lanes].astype(F32) * attended.astype(F32)
            delta = jnp.sum(head_rows(prod, lane_head), axis=1, keepdims=True)
            deltas.append(delta)
            scales.append(scale)
            cols = jnp.where(lane == 2 * unit, tops[unit] + jnp.log(totals[unit]), cols)
            cols = jnp.where(lane == 2 * unit + 1, delta, cols)
        for unit, (slot, pair) in enumerate(units):
            for start in range(0, 2 * tokens, CHUNK):
                part = slice(start, start + CHUNK)
                grad_scores = s_scr[unit, part, :] * (d_scr[unit, part, :] - deltas[unit][part])
                p_scr[unit, part, :] = grad_scores.astype(BF16)
        for unit, (slot, pair) in enumerate(units):
            lanes, kind = lanes_of[pair], kinds[slot]
            wide = nn(p_scr[unit], keys.window(kind, lanes)) * (scales[unit] * SCALE)
            grad_q = head_lanes(wide, lane_head).astype(BF16)
            dq[slot_of(row_of(kind, rows)), :, :, lanes] = grad_q.reshape(columns, frames, PAIR)
        turned = cols.T
        for unit, (slot, pair) in enumerate(units):
            for which in range(2):
                line = turned[2 * unit + which : 2 * unit + which + 1]
                for h in range(2):
                    to = which * 2 * PAIRS + pair * 2 + h
                    stats[len(carried) + slot, group, to : to + 1, :] = line[:, h * tokens : (h + 1) * tokens]
        return 0

    lax.fori_loop(0, width // PART, step, 0)


def backward_kernel(layout, kinds, *refs):
    n_in, count = layout["n_in"], layout["count"]
    kv = refs[0]
    qgs, stats_of = refs[1 : 1 + count], refs[1 + count : 1 + 2 * count]
    rims = refs[1 + 2 * count : n_in]
    mask, *outs = refs[n_in:-4]
    s_scr, d_scr, p_scr, t_scr = refs[-4:]
    rows = kv.shape[0] // 2
    copies = []
    if layout.get("held"):
        sems = refs[-5]
        for at, (held, out) in enumerate(zip(refs[n_in - 2 : n_in], outs[1:3])):
            copies.append(pltpu.make_async_copy(held, out, sems.at[at]))
            copies[-1].start()
    tokens, width = kv.shape[1:]
    part = count * tokens
    lane_head = lax.broadcasted_iota(jnp.int32, (tokens, PAIR), 1) // HEAD_DIM
    units = [(kind, pair) for kind in kinds for pair in range(PAIRS)]

    def query_rows(kind):
        inner = rows - 2
        if isinstance(kind, int):
            first, _ = edge_rows(rows)
            out = []
            for row in (kind - 1, kind, kind + 1):
                if 0 < row < rows - 1:
                    out.append((row, row - 1))
                else:
                    out.append((row, jnp.where(first == row, inner, inner + 1)))
            return out
        side = int(kind[-1])
        edge = edge_rows(rows)[side]
        if kind[0] == "r":
            return [(edge, inner + side)]
        near = jnp.where(edge == 0, 1, edge - 1)
        return [(edge, inner + side), (near, near - 1)]

    def key_rows(kind, tensor, lanes):
        if isinstance(kind, int):
            return kv[tensor * rows + kind, :, lanes]
        side = int(kind[-1])
        if kind[0] == "r":
            return rims[side][tensor, :, lanes]
        return kv[tensor * rows + edge_rows(rows)[side], :, lanes]

    def window(kind, tensor, lanes):
        found = [qg[tensor * rows + row, :, lanes] for row, _ in query_rows(kind) for qg in qgs]
        return jnp.concatenate(found, axis=0)

    def products(group):
        for unit, (kind, pair) in enumerate(units):
            lanes = lanes_at(group, pair)
            size = len(query_rows(kind)) * part
            at = (group % 2) * len(units) + unit
            s_scr[at, :, :size] = nt(
                head_rows(key_rows(kind, 0, lanes) * SCALE, lane_head), window(kind, 0, lanes)
            )
            d_scr[at, :, :size] = nt(
                head_rows(key_rows(kind, 1, lanes), lane_head), window(kind, 1, lanes)
            )

    def finish(group):
        base = (group % 2) * len(units)
        stats = {
            kind: jnp.concatenate(
                [ref[slot, group] for _, slot in query_rows(kind) for ref in stats_of], axis=1
            )
            for kind in kinds
        }
        for unit, (kind, pair) in enumerate(units):
            stat = stats[kind]
            size = stat.shape[1]
            bias = jnp.concatenate([mask[0, 0:1]] * (size // part), axis=1)
            for h in range(2):
                at = pair * 2 + h
                lse = stat[at : at + 1] + bias
                delta = stat[2 * PAIRS + at : 2 * PAIRS + at + 1]
                for start in range(h * tokens, (h + 1) * tokens, CHUNK):
                    rows_at = slice(start, start + CHUNK)
                    probs = jnp.exp(s_scr[base + unit, rows_at, :size] - lse)
                    p_scr[base + unit, rows_at, :size] = probs.astype(BF16)
                    grad_scores = probs * (d_scr[base + unit, rows_at, :size] - delta)
                    t_scr[base + unit, rows_at, :size] = grad_scores.astype(BF16)
        for unit, (kind, pair) in enumerate(units):
            lanes = lanes_at(group, pair)
            size = len(query_rows(kind)) * part
            grad_v = head_lanes(nn(p_scr[base + unit, :, :size], window(kind, 1, lanes)), lane_head)
            grad_k = head_lanes(nn(t_scr[base + unit, :, :size], window(kind, 0, lanes)), lane_head) * SCALE
            for tensor, value in enumerate((grad_k, grad_v)):
                if isinstance(kind, str) and kind[0] == "r":
                    outs[int(kind[-1])][tensor, :, lanes] = value.astype(BF16)
                else:
                    row = row_of(kind, rows)
                    outs[0][tensor * rows + row, :, lanes] = value

    products(0)
    for group in range(width // PART):
        if group + 1 < width // PART:
            products(group + 1)
        finish(group)
    for copy in copies:
        copy.wait()


def finish_kernel(total, part0, part1, dk, dv, dk_held, dv_held, sems):
    rows, columns, frames, width = dk.shape
    copies = []

    def send(tensor, row, value):
        held, out = ((dk_held, dk), (dv_held, dv))[tensor]
        held[row] = value.astype(BF16).reshape(columns, frames, width)
        copies.append(pltpu.make_async_copy(held.at[row], out.at[row], sems.at[len(copies)]))
        copies[-1].start()

    for tensor in range(2):
        for row in range(1, rows - 1):
            send(tensor, row, total[tensor * rows + row])
        for part, row in zip((part0, part1), edge_rows(rows)):
            send(tensor, row, total[tensor * rows + row] + part[tensor].astype(F32))
    for copy in copies:
        copy.wait()


def per_device(query_vectors, key_vectors, value_vectors, out_cotangent, partner_mask):
    frames, rows, columns, width = query_vectors.shape
    bits = min(4, lax.axis_size("frame").bit_length() - 1)
    count = bits + 1
    tokens = frames * columns
    groups = width // PART
    window = 3 * count * tokens
    table = partner_mask.T
    turn = lambda a: jnp.transpose(a, (1, 2, 0, 3))
    back = lambda a: jnp.transpose(a, (2, 0, 1, 3))

    kv, kv_edge0, kv_edge1 = pack([turn(key_vectors), turn(value_vectors)])
    kvs = [kv] + swaps(kv, bits)
    kv_rims = [exchange(kv_edge0, 0), exchange(kv_edge1, 1)]
    mask = lambda n: struct(n, 8, count * tokens, dtype=F32)
    mask_f, mask_b = call(functools.partial(mask_kernel, count, frames), [mask(3), mask(1)], [kv_edge0], table=table)
    joined, k_joined = join(kv_rims, [mask_b])
    core_rims = swap(joined, 0)
    k_rims_of = [swap(k_joined, bit) for bit in range(1, bits)]
    qg, _, _ = pack([turn(query_vectors), turn(out_cotangent)], [kv_edge0])
    qgs = [qg] + swaps(qg, bits)
    v_far = [exchange(e, side) for side, e in enumerate(value_edges(kvs[2:]))]

    inner_kinds = list(range(1, rows - 1))
    edge_kinds = ["0", "1"]
    inner = len(inner_kinds)
    work = 4 * 2 * (width // PAIR) * 2 * tokens * window * PAIR
    exps = (width // HEAD_DIM) * tokens * window
    line = lambda n: struct(n, columns, frames, width)

    def scratches(n, extra):
        wide = [pltpu.VMEM((n, 2 * tokens, window), F32)] * 2
        return wide + [pltpu.VMEM((n, 2 * tokens, window), BF16)] * extra

    def gathered(at, rim_at, tensor):
        mids = [(at + block, tensor * rows) for block in range(count)]
        if rim_at is None:
            return mids, []
        sides = []
        for side in range(2):
            near = [(rim_at + side, tensor), (rim_at + 2, 2 * side + tensor)]
            if tensor == 0:
                far = [(rim_at + 3 + at, side) for at in range(bits - 1)]
            else:
                far = [(rim_at + 2 + bits + side, at) for at in range(bits - 1)]
            sides.append(near + far)
        return mids, sides

    stat = lambda n: struct(n, groups, 4 * PAIRS, tokens, dtype=F32)
    ins = [qg] + kvs
    layout = {"n_in": len(ins), "own": 0, "k": gathered(1, None, 0), "v": gathered(1, None, 1)}
    inner_out = call(
        functools.partial(forward_kernel, layout, inner_kinds, ()),
        [line(inner), line(inner), stat(inner)], ins + [mask_f],
        flops=work * inner, exps=exps * inner, scratch=scratches(RING, 2), limit=14 << 20,
    )
    rim_at = len(ins)
    ins = ins + kv_rims + [core_rims] + k_rims_of + v_far + list(inner_out)
    layout = {"n_in": len(ins), "own": 0, "k": gathered(1, rim_at, 0), "v": gathered(1, rim_at, 1)}
    attended, dq, stats = call(
        functools.partial(forward_kernel, layout, edge_kinds, inner_kinds),
        [line(rows), line(rows), stat(rows)], ins + [mask_f],
        flops=work * 2, exps=exps * 2, scratch=scratches(RING, 2), limit=14 << 20,
    )
    ss = [stats] + swaps(stats, bits)

    ins = [kv] + qgs + ss + kv_rims
    layout = {"n_in": len(ins), "count": count, "frames": frames}
    edge = struct(2, tokens, width)
    parts = call(
        functools.partial(backward_kernel, layout, ["r0", "r1"]),
        [edge, edge], ins + [mask_b],
        flops=work, exps=exps, scratch=scratches(4 * PAIRS, 2), limit=14 << 20,
    )
    parts = [exchange(value, side) for side, value in enumerate(parts)]
    full = struct(rows, columns, frames, width)
    ins = ins + [attended, dq]
    layout = {"n_in": len(ins), "count": count, "frames": frames, "held": 2}
    total, attended, dq = call(
        functools.partial(backward_kernel, layout, inner_kinds + edge_kinds),
        [struct(2 * rows, tokens, width, dtype=F32), full, full], ins + [mask_b], to_hbm=(1, 2),
        flops=2 * work, exps=2 * exps, limit=18 << 20,
        scratch=[pltpu.SemaphoreType.DMA((2,))] + scratches(2 * rows * PAIRS, 2),
    )
    dk, dv = call(
        finish_kernel, [full, full], [total] + parts, to_hbm=(0, 1),
        scratch=[pltpu.VMEM(full.shape, BF16)] * 2 + [pltpu.SemaphoreType.DMA((2 * rows,))],
    )
    return back(attended), back(dq), back(dk), back(dv)


def solution(mesh):
    spec = P("frame", "space", None, None)

    return jax.shard_map(
        per_device,
        mesh=mesh,
        in_specs=(spec, spec, spec, spec, P()),
        out_specs=(spec, spec, spec, spec),
        check_vma=False,
    )
```

```python
import functools

import jax
import jax.numpy as jnp
from jax import lax
from jax.experimental import pallas as pl
from jax.experimental.pallas import tpu as pltpu
from jax.sharding import PartitionSpec as P


HEAD_DIM = 64
SCALE = 0.125
NEG = -1e30
PAIR = 2 * HEAD_DIM
PAIRS = 2
PART = PAIRS * PAIR
CHUNK = 16
RING = 4
BF16 = jnp.bfloat16
F32 = jnp.float32


def swap(value, bit):
    size = lax.axis_size("frame")
    return lax.ppermute(value, "frame", [(i, i ^ 1 << bit) for i in range(size)])


def swaps(value, bits):
    return [swap(value, bit) for bit in range(bits)]


def exchange(value, side):
    pairs = []
    for low in range(side, lax.axis_size("space") - 1, 2):
        pairs += [(low, low + 1), (low + 1, low)]
    return lax.ppermute(value, "space", pairs)


def struct(*shape, dtype=BF16):
    return jax.ShapeDtypeStruct(shape, dtype)


def call(kernel, outs, ins, flops=0, exps=0, scratch=(), limit=4 << 20, table=None, to_hbm=(), raw=0):
    size = sum(a.size * a.dtype.itemsize for a in ins) + sum(
        o.size * jnp.dtype(o.dtype).itemsize for o in outs
    )
    ins = [pltpu.with_memory_space_constraint(a, pltpu.HBM) for a in ins[:raw]] + [pltpu.with_memory_space_constraint(a, pltpu.VMEM) for a in ins[raw:]]
    specs = [pl.BlockSpec(memory_space=pltpu.HBM if i < raw else pltpu.VMEM) for i in range(len(ins))]
    if table is not None:
        ins = ins + [table]
        specs = specs + [pl.BlockSpec(memory_space=pltpu.SMEM)]
    return pl.pallas_call(
        kernel,
        out_shape=tuple(
            o if i in to_hbm else pltpu.VMEM(o.shape, o.dtype) for i, o in enumerate(outs)
        ),
        in_specs=specs,
        out_specs=tuple(
            pl.BlockSpec(memory_space=pl.ANY if i in to_hbm else pltpu.VMEM) for i in range(len(outs))
        ),
        scratch_shapes=list(scratch),
        compiler_params=pltpu.CompilerParams(vmem_limit_bytes=limit),
        cost_estimate=pl.CostEstimate(flops=flops, bytes_accessed=size, transcendentals=exps),
    )(*ins)


def edge_rows(rows):
    odd = lax.rem(lax.axis_index("space"), 2)
    return (rows - 1) * (1 - odd), (rows - 1) * odd


def pack_kernel(n, *refs):
    sources, (packed, edge0, edge1, *held, sems) = refs[:n], refs[-4 - n :]
    rows, columns, frames, width = sources[0].shape
    flat = (columns * frames, width)
    copies = [
        [pltpu.make_async_copy(source.at[row], held[at].at[row], sems.at[at, row]) for row in range(rows)]
        for at, source in enumerate(sources)
    ]
    for copy in sum(copies, []):
        copy.start()
    for at in range(n):
        for row in range(rows):
            copies[at][row].wait()
            packed[at * rows + row] = held[at][row].reshape(flat)
    for edge, row in zip((edge0, edge1), edge_rows(rows)):
        for at in range(n):
            edge[at] = packed[at * rows + row]


def pack(sources, after=()):
    n = len(sources)
    rows, columns, frames, width = sources[0].shape
    edge = struct(n, columns * frames, width)
    outs = [struct(n * rows, columns * frames, width), edge, edge]
    kernel = functools.partial(pack_kernel, n)
    held = [pltpu.VMEM(s.shape, s.dtype) for s in sources]
    scratch = held + [pltpu.SemaphoreType.DMA((n, rows))]
    return call(kernel, outs, sources + list(after), scratch=scratch, raw=n)


def join_kernel(side0, side1, after, both, keys):
    for side, source in enumerate((side0, side1)):
        both[2 * side] = source[0]
        both[2 * side + 1] = source[1]
        keys[side] = source[0]


def join(sources, after):
    shape = sources[0].shape[1:]
    return call(join_kernel, [struct(4, *shape), struct(2, *shape)], sources + after)


def edge_kernel(*refs):
    sources, targets = refs[:-2], refs[-2:]
    rows = sources[0].shape[0] // 2
    for slot, source in enumerate(sources):
        for target, row in zip(targets, edge_rows(rows)):
            target[slot] = source[rows + row]


def value_edges(sources):
    edge = struct(len(sources), *sources[0].shape[1:])
    return call(edge_kernel, [edge, edge], sources)


def lanes_at(group, pair):
    start = group * PART + pair * PAIR
    return slice(start, start + PAIR)


def head_rows(value, lane_head):
    zero = jnp.zeros_like(value)
    return jnp.concatenate([jnp.where(lane_head == h, value, zero) for h in range(2)], axis=0)


def head_lanes(stacked, lane_head):
    tokens = stacked.shape[0] // 2
    return jnp.where(lane_head == 0, stacked[:tokens], stacked[tokens:])


def nt(a, b):
    return lax.dot_general(a, b, (((1,), (1,)), ((), ())), preferred_element_type=F32)


def nn(a, b):
    return jnp.dot(a, b, preferred_element_type=F32)


class Pieces:
    def __init__(self, refs, rows, mids, rim_slots):
        self.rows = rows
        self.mids = [(refs[i], s) for i, s in mids]
        self.rims = [[(refs[i], s) for i, s in side] for side in rim_slots]

    def window(self, kind, lanes):
        out = []
        for at in range(3):
            for block, (mid, base) in enumerate(self.mids):
                if isinstance(kind, int):
                    out.append(mid[base + kind - 1 + at, :, lanes])
                elif at == 0:
                    ref, slot = self.rims[int(kind)][block]
                    out.append(ref[slot, :, lanes])
                else:
                    edge = edge_rows(self.rows)[int(kind)]
                    inner = jnp.where(edge == 0, 1, edge - 1)
                    out.append(mid[base + (edge if at == 1 else inner), :, lanes])
        return jnp.concatenate(out, axis=0)


def row_of(kind, rows):
    return kind if isinstance(kind, int) else edge_rows(rows)[int(kind)]


def rim_open(side):
    band, size = lax.axis_index("space"), lax.axis_size("space")
    odd = lax.rem(band, 2)
    up = (odd == 0) if side == 0 else (odd == 1)
    other = jnp.where(up, band + 1, band - 1)
    return (other >= 0) & (other < size)


def build_masks(mask_ref, blocks, frames, table, queries_here):
    shape = mask_ref.shape[1:]
    tokens = shape[1] // blocks
    lane = lax.broadcasted_iota(jnp.int32, shape, 1)
    sub = lax.broadcasted_iota(jnp.int32, shape, 0)
    bad = NEG if queries_here else -NEG
    which = sub if queries_here else lane
    which = lax.rem(which, frames)
    group = lane // tokens
    here = lax.axis_index("frame")
    value = jnp.zeros(shape, F32)
    for block in range(1, blocks):
        owner = here if queries_here else jnp.bitwise_xor(here, 1 << (block - 1))
        for frame in range(frames):
            off = jnp.where(table[block - 1, owner * frames + frame] == 1, 0.0, bad)
            value = jnp.where((group == block) & (which == frame), off.astype(F32), value)
    mask_ref[0] = value
    if queries_here:
        for side in range(2):
            mask_ref[1 + side] = value + jnp.where(rim_open(side), 0.0, bad).astype(F32)


def mask_kernel(blocks, frames, after, table, mask_f, mask_b):
    build_masks(mask_f, blocks, frames, table, True)
    build_masks(mask_b, blocks, frames, table, False)


def forward_kernel(layout, kinds, carried, *refs):
    qg = refs[layout["own"]]
    rows = qg.shape[0] // 2
    keys, values = (Pieces(refs, rows, *layout[name]) for name in ("k", "v"))
    n_in = layout["n_in"]
    mask = refs[n_in]
    out, dq, stats = refs[n_in + 1 :][:3]
    s_scr, d_scr, p_scr, _ = refs[-4:]
    tokens, width = qg.shape[1:]
    columns, frames = out.shape[1:3]
    if carried:
        for target, source in zip((out, dq), refs[n_in - 3 : n_in - 1]):
            for at, row in enumerate(carried):
                target[row] = source[at]
        for at in range(len(carried)):
            stats[at] = refs[n_in - 1][at]
    lane_head = lax.broadcasted_iota(jnp.int32, (tokens, PAIR), 1) // HEAD_DIM
    lane = lax.broadcasted_iota(jnp.int32, (2 * tokens, 128), 1)
    slot_of = lambda row: row if carried else row - 1
    units = [(slot, pair) for slot in range(len(kinds)) for pair in range(PAIRS)]

    def step(group, _):
        starts = [pl.multiple_of(group * PART + pair * PAIR, PAIR) for pair in range(PAIRS)]
        lanes_of = [pl.ds(start, PAIR) for start in starts]
        for unit, (slot, pair) in enumerate(units):
            lanes, kind = lanes_of[pair], kinds[slot]
            row = row_of(kind, rows)
            s_scr[unit] = nt(head_rows(qg[row, :, lanes] * SCALE, lane_head), keys.window(kind, lanes))
            d_scr[unit] = nt(head_rows(qg[rows + row, :, lanes], lane_head), values.window(kind, lanes))
        tops, totals = [], []
        for unit, (slot, pair) in enumerate(units):
            top_parts, total_parts = [], []
            first = mask[0] if isinstance(kinds[slot], int) else mask[1 + int(kinds[slot])]
            bias = jnp.concatenate([first, mask[0], mask[0]], axis=1)
            bias = jnp.concatenate([bias] * (CHUNK // 8), axis=0)
            for start in range(0, 2 * tokens, CHUNK):
                scores = s_scr[unit, start : start + CHUNK, :] + bias
                top = jnp.max(scores, axis=1, keepdims=True)
                raw = jnp.exp(scores - top)
                s_scr[unit, start : start + CHUNK, :] = raw
                p_scr[unit, start : start + CHUNK, :] = raw.astype(BF16)
                top_parts.append(top)
                total_parts.append(jnp.sum(raw, axis=1, keepdims=True))
            tops.append(jnp.concatenate(top_parts, axis=0))
            totals.append(jnp.concatenate(total_parts, axis=0))
        cols = jnp.zeros((2 * tokens, 128), F32)
        deltas, scales = [], []
        for unit, (slot, pair) in enumerate(units):
            lanes, kind = lanes_of[pair], kinds[slot]
            row = row_of(kind, rows)
            scale = 1.0 / totals[unit]
            wide = nn(p_scr[unit], values.window(kind, lanes)) * scale
            attended = head_lanes(wide, lane_head).astype(BF16)
            out[slot_of(row), :, :, lanes] = attended.reshape(columns, frames, PAIR)
            prod = qg[rows + row, :, lanes].astype(F32) * attended.astype(F32)
            delta = jnp.sum(head_rows(prod, lane_head), axis=1, keepdims=True)
            deltas.append(delta)
            scales.append(scale)
            cols = jnp.where(lane == 2 * unit, tops[unit] + jnp.log(totals[unit]), cols)
            cols = jnp.where(lane == 2 * unit + 1, delta, cols)
        for unit, (slot, pair) in enumerate(units):
            for start in range(0, 2 * tokens, CHUNK):
                part = slice(start, start + CHUNK)
                grad_scores = s_scr[unit, part, :] * (d_scr[unit, part, :] - deltas[unit][part])
                p_scr[unit, part, :] = grad_scores.astype(BF16)
        for unit, (slot, pair) in enumerate(units):
            lanes, kind = lanes_of[pair], kinds[slot]
            wide = nn(p_scr[unit], keys.window(kind, lanes)) * (scales[unit] * SCALE)
            grad_q = head_lanes(wide, lane_head).astype(BF16)
            dq[slot_of(row_of(kind, rows)), :, :, lanes] = grad_q.reshape(columns, frames, PAIR)
        turned = cols.T
        for unit, (slot, pair) in enumerate(units):
            for which in range(2):
                line = turned[2 * unit + which : 2 * unit + which + 1]
                for h in range(2):
                    to = which * 2 * PAIRS + pair * 2 + h
                    stats[len(carried) + slot, group, to : to + 1, :] = line[:, h * tokens : (h + 1) * tokens]
        return 0

    lax.fori_loop(0, width // PART, step, 0)


def forward_edge_kernel(layout, kinds, carried, *refs):
    qg = refs[layout["own"]]
    rows = qg.shape[0] // 2
    keys, values = (Pieces(refs, rows, *layout[name]) for name in ("k", "v"))
    n_in = layout["n_in"]
    mask = refs[n_in]
    out, stats, raw_out, column_out = refs[n_in + 1 :][:4]
    s_scr, p_scr = refs[-2:]
    tokens, width = qg.shape[1:]
    columns, frames = out.shape[1:3]
    if carried:
        for at, row in enumerate(carried):
            out[row] = refs[n_in - 2][at]
            stats[at] = refs[n_in - 1][at]
    lane_head = lax.broadcasted_iota(jnp.int32, (tokens, PAIR), 1) // HEAD_DIM
    lane = lax.broadcasted_iota(jnp.int32, (2 * tokens, 128), 1)
    slot_of = lambda row: row if carried else row - 1
    units = [(slot, pair) for slot in range(len(kinds)) for pair in range(PAIRS)]

    def step(group, _):
        starts = [pl.multiple_of(group * PART + pair * PAIR, PAIR) for pair in range(PAIRS)]
        lanes_of = [pl.ds(start, PAIR) for start in starts]
        for unit, (slot, pair) in enumerate(units):
            lanes, kind = lanes_of[pair], kinds[slot]
            row = row_of(kind, rows)
            s_scr[unit] = nt(head_rows(qg[row, :, lanes] * SCALE, lane_head), keys.window(kind, lanes))
        tops, totals = [], []
        for unit, (slot, pair) in enumerate(units):
            top_parts, total_parts = [], []
            first = mask[0] if isinstance(kinds[slot], int) else mask[1 + int(kinds[slot])]
            bias = jnp.concatenate([first, mask[0], mask[0]], axis=1)
            bias = jnp.concatenate([bias] * (CHUNK // 8), axis=0)
            for start in range(0, 2 * tokens, CHUNK):
                scores = s_scr[unit, start : start + CHUNK, :] + bias
                top = jnp.max(scores, axis=1, keepdims=True)
                raw = jnp.exp(scores - top)
                raw_out[group * len(units) + unit, start : start + CHUNK, :] = raw
                p_scr[unit, start : start + CHUNK, :] = raw.astype(BF16)
                top_parts.append(top)
                total_parts.append(jnp.sum(raw, axis=1, keepdims=True))
            tops.append(jnp.concatenate(top_parts, axis=0))
            totals.append(jnp.concatenate(total_parts, axis=0))
        cols = jnp.zeros((2 * tokens, 128), F32)
        for unit, (slot, pair) in enumerate(units):
            lanes, kind = lanes_of[pair], kinds[slot]
            row = row_of(kind, rows)
            scale = 1.0 / totals[unit]
            wide = nn(p_scr[unit], values.window(kind, lanes)) * scale
            attended = head_lanes(wide, lane_head).astype(BF16)
            out[slot_of(row), :, :, lanes] = attended.reshape(columns, frames, PAIR)
            prod = qg[rows + row, :, lanes].astype(F32) * attended.astype(F32)
            delta = jnp.sum(head_rows(prod, lane_head), axis=1, keepdims=True)
            for which, column in enumerate((scale, delta)):
                column_out[group * len(units) + unit, which] = jnp.broadcast_to(column, (2 * tokens, 128))
            cols = jnp.where(lane == 2 * unit, tops[unit] + jnp.log(totals[unit]), cols)
            cols = jnp.where(lane == 2 * unit + 1, delta, cols)
        turned = cols.T
        for unit, (slot, pair) in enumerate(units):
            for which in range(2):
                line = turned[2 * unit + which : 2 * unit + which + 1]
                for h in range(2):
                    to = which * 2 * PAIRS + pair * 2 + h
                    stats[len(carried) + slot, group, to : to + 1, :] = line[:, h * tokens : (h + 1) * tokens]
        return 0

    lax.fori_loop(0, width // PART, step, 0)


def forward_grad_kernel(layout, kinds, carried, *refs):
    qg = refs[layout["own"]]
    rows = qg.shape[0] // 2
    keys, values = (Pieces(refs, rows, *layout[name]) for name in ("k", "v"))
    n_in = layout["n_in"]
    inner_dq, raw_in, column_in = refs[n_in - 3 : n_in]
    dq, d_scr, p_scr = refs[n_in:]
    tokens, width = qg.shape[1:]
    columns, frames = dq.shape[1:3]
    window = d_scr.shape[2]
    for at, row in enumerate(carried):
        dq[row] = inner_dq[at]
    lane_head = lax.broadcasted_iota(jnp.int32, (tokens, PAIR), 1) // HEAD_DIM
    units = [(slot, pair) for slot in range(len(kinds)) for pair in range(PAIRS)]

    def products(group):
        for unit, (slot, pair) in enumerate(units):
            lanes, kind = lanes_at(group, pair), kinds[slot]
            row = row_of(kind, rows)
            at = (group % 2) * len(units) + unit
            d_scr[at] = nt(head_rows(qg[rows + row, :, lanes], lane_head), values.window(kind, lanes))

    def finish(group):
        base = (group % 2) * len(units)
        for unit, (slot, pair) in enumerate(units):
            held = group * len(units) + unit
            for start in range(0, 2 * tokens, CHUNK):
                part = slice(start, start + CHUNK)
                delta = column_in[held, 1, part, :]
                for low in range(0, window, 128):
                    size = min(128, window - low)
                    span = slice(low, low + size)
                    value = raw_in[held, part, span] * (d_scr[base + unit, part, span] - delta[:, :size])
                    p_scr[base + unit, part, span] = value.astype(BF16)
        for unit, (slot, pair) in enumerate(units):
            lanes, kind = lanes_at(group, pair), kinds[slot]
            scale = column_in[group * len(units) + unit, 0] * SCALE
            wide = nn(p_scr[base + unit], keys.window(kind, lanes)) * scale
            grad_q = head_lanes(wide, lane_head).astype(BF16)
            dq[row_of(kind, rows), :, :, lanes] = grad_q.reshape(columns, frames, PAIR)

    products(0)
    for group in range(width // PART):
        if group + 1 < width // PART:
            products(group + 1)
        finish(group)


def backward_kernel(layout, kinds, *refs):
    n_in, count = layout["n_in"], layout["count"]
    kv = refs[0]
    qgs, stats_of = refs[1 : 1 + count], refs[1 + count : 1 + 2 * count]
    rims = refs[1 + 2 * count : n_in]
    mask, *outs = refs[n_in:-4]
    s_scr, d_scr, p_scr, t_scr = refs[-4:]
    rows = kv.shape[0] // 2
    copies = []
    if layout.get("held"):
        sems = refs[-5]
        for at, (held, out) in enumerate(zip(refs[n_in - 2 : n_in], outs[1:3])):
            copies.append(pltpu.make_async_copy(held, out, sems.at[at]))
            copies[-1].start()
    tokens, width = kv.shape[1:]
    part = count * tokens
    lane_head = lax.broadcasted_iota(jnp.int32, (tokens, PAIR), 1) // HEAD_DIM
    units = [(kind, pair) for kind in kinds for pair in range(PAIRS)]

    def query_rows(kind):
        inner = rows - 2
        if isinstance(kind, int):
            first, _ = edge_rows(rows)
            out = []
            for row in (kind - 1, kind, kind + 1):
                if 0 < row < rows - 1:
                    out.append((row, row - 1))
                else:
                    out.append((row, jnp.where(first == row, inner, inner + 1)))
            return out
        side = int(kind[-1])
        edge = edge_rows(rows)[side]
        if kind[0] == "r":
            return [(edge, inner + side)]
        near = jnp.where(edge == 0, 1, edge - 1)
        return [(edge, inner + side), (near, near - 1)]

    def key_rows(kind, tensor, lanes):
        if isinstance(kind, int):
            return kv[tensor * rows + kind, :, lanes]
        side = int(kind[-1])
        if kind[0] == "r":
            return rims[side][tensor, :, lanes]
        return kv[tensor * rows + edge_rows(rows)[side], :, lanes]

    def window(kind, tensor, lanes):
        found = [qg[tensor * rows + row, :, lanes] for row, _ in query_rows(kind) for qg in qgs]
        return jnp.concatenate(found, axis=0)

    def products(group):
        for unit, (kind, pair) in enumerate(units):
            lanes = lanes_at(group, pair)
            size = len(query_rows(kind)) * part
            at = (group % 2) * len(units) + unit
            s_scr[at, :, :size] = nt(
                head_rows(key_rows(kind, 0, lanes) * SCALE, lane_head), window(kind, 0, lanes)
            )
            d_scr[at, :, :size] = nt(
                head_rows(key_rows(kind, 1, lanes), lane_head), window(kind, 1, lanes)
            )

    def finish(group):
        base = (group % 2) * len(units)
        stats = {
            kind: jnp.concatenate(
                [ref[slot, group] for _, slot in query_rows(kind) for ref in stats_of], axis=1
            )
            for kind in kinds
        }
        for unit, (kind, pair) in enumerate(units):
            stat = stats[kind]
            size = stat.shape[1]
            bias = jnp.concatenate([mask[0, 0:1]] * (size // part), axis=1)
            for h in range(2):
                at = pair * 2 + h
                lse = stat[at : at + 1] + bias
                delta = stat[2 * PAIRS + at : 2 * PAIRS + at + 1]
                for start in range(h * tokens, (h + 1) * tokens, CHUNK):
                    rows_at = slice(start, start + CHUNK)
                    probs = jnp.exp(s_scr[base + unit, rows_at, :size] - lse)
                    p_scr[base + unit, rows_at, :size] = probs.astype(BF16)
                    grad_scores = probs * (d_scr[base + unit, rows_at, :size] - delta)
                    t_scr[base + unit, rows_at, :size] = grad_scores.astype(BF16)
        for unit, (kind, pair) in enumerate(units):
            lanes = lanes_at(group, pair)
            size = len(query_rows(kind)) * part
            grad_v = head_lanes(nn(p_scr[base + unit, :, :size], window(kind, 1, lanes)), lane_head)
            grad_k = head_lanes(nn(t_scr[base + unit, :, :size], window(kind, 0, lanes)), lane_head) * SCALE
            for tensor, value in enumerate((grad_k, grad_v)):
                if isinstance(kind, str) and kind[0] == "r":
                    outs[int(kind[-1])][tensor, :, lanes] = value.astype(BF16)
                else:
                    row = row_of(kind, rows)
                    outs[0][tensor * rows + row, :, lanes] = value

    products(0)
    for group in range(width // PART):
        if group + 1 < width // PART:
            products(group + 1)
        finish(group)
    for copy in copies:
        copy.wait()


def finish_kernel(total, part0, part1, dk, dv, dk_held, dv_held, sems):
    rows, columns, frames, width = dk.shape
    copies = []

    def send(tensor, row, value):
        held, out = ((dk_held, dk), (dv_held, dv))[tensor]
        held[row] = value.astype(BF16).reshape(columns, frames, width)
        copies.append(pltpu.make_async_copy(held.at[row], out.at[row], sems.at[len(copies)]))
        copies[-1].start()

    for tensor in range(2):
        for row in range(1, rows - 1):
            send(tensor, row, total[tensor * rows + row])
        for part, row in zip((part0, part1), edge_rows(rows)):
            send(tensor, row, total[tensor * rows + row] + part[tensor].astype(F32))
    for copy in copies:
        copy.wait()


def per_device(query_vectors, key_vectors, value_vectors, out_cotangent, partner_mask):
    frames, rows, columns, width = query_vectors.shape
    bits = min(4, lax.axis_size("frame").bit_length() - 1)
    count = bits + 1
    tokens = frames * columns
    groups = width // PART
    window = 3 * count * tokens
    table = partner_mask.T
    turn = lambda a: jnp.transpose(a, (1, 2, 0, 3))
    back = lambda a: jnp.transpose(a, (2, 0, 1, 3))

    kv, kv_edge0, kv_edge1 = pack([turn(key_vectors), turn(value_vectors)])
    kvs = [kv] + swaps(kv, bits)
    kv_rims = [exchange(kv_edge0, 0), exchange(kv_edge1, 1)]
    mask = lambda n: struct(n, 8, count * tokens, dtype=F32)
    mask_f, mask_b = call(functools.partial(mask_kernel, count, frames), [mask(3), mask(1)], [kv_edge0], table=table)
    joined, k_joined = join(kv_rims, [mask_b])
    core_rims = swap(joined, 0)
    k_rims_of = [swap(k_joined, bit) for bit in range(1, bits)]
    qg, _, _ = pack([turn(query_vectors), turn(out_cotangent)], [kv_edge0])
    qgs = [qg] + swaps(qg, bits)
    v_far = [exchange(e, side) for side, e in enumerate(value_edges(kvs[2:]))]

    inner_kinds = list(range(1, rows - 1))
    edge_kinds = ["0", "1"]
    inner = len(inner_kinds)
    work = 4 * 2 * (width // PAIR) * 2 * tokens * window * PAIR
    exps = (width // HEAD_DIM) * tokens * window
    line = lambda n: struct(n, columns, frames, width)

    def scratches(n, extra):
        wide = [pltpu.VMEM((n, 2 * tokens, window), F32)] * 2
        return wide + [pltpu.VMEM((n, 2 * tokens, window), BF16)] * extra

    def gathered(at, rim_at, tensor):
        mids = [(at + block, tensor * rows) for block in range(count)]
        if rim_at is None:
            return mids, []
        sides = []
        for side in range(2):
            near = [(rim_at + side, tensor), (rim_at + 2, 2 * side + tensor)]
            if tensor == 0:
                far = [(rim_at + 3 + at, side) for at in range(bits - 1)]
            else:
                far = [(rim_at + 2 + bits + side, at) for at in range(bits - 1)]
            sides.append(near + far)
        return mids, sides

    stat = lambda n: struct(n, groups, 4 * PAIRS, tokens, dtype=F32)
    ins = [qg] + kvs
    layout = {"n_in": len(ins), "own": 0, "k": gathered(1, None, 0), "v": gathered(1, None, 1)}
    inner_out = call(
        functools.partial(forward_kernel, layout, inner_kinds, ()),
        [line(inner), line(inner), stat(inner)], ins + [mask_f],
        flops=work * inner, exps=exps * inner, scratch=scratches(RING, 2), limit=14 << 20,
    )
    rim_at = len(ins)
    inner_att, inner_dq, inner_stats = inner_out
    base = ins + kv_rims + [core_rims] + k_rims_of + v_far
    found = {"own": 0, "k": gathered(1, rim_at, 0), "v": gathered(1, rim_at, 1)}
    ins = base + [inner_att, inner_stats]
    layout = {"n_in": len(ins), **found}
    jobs = groups * PAIRS * 2
    kept = [struct(jobs, 2 * tokens, window, dtype=F32), struct(jobs, 2, 2 * tokens, 128, dtype=F32)]
    piece = lambda n, dtype: pltpu.VMEM((n, 2 * tokens, window), dtype)
    attended, stats, *kept = call(
        functools.partial(forward_edge_kernel, layout, edge_kinds, inner_kinds),
        [line(rows), stat(rows)] + kept, ins + [mask_f],
        flops=work, exps=exps * 2, scratch=[piece(2 * PAIRS, F32), piece(2 * PAIRS, BF16)], limit=10 << 20,
    )
    ins = base + [inner_dq] + kept
    layout = {"n_in": len(ins), **found}
    (dq,) = call(
        functools.partial(forward_grad_kernel, layout, edge_kinds, inner_kinds),
        [line(rows)], ins,
        flops=work, scratch=[piece(4 * PAIRS, F32), piece(4 * PAIRS, BF16)], limit=10 << 20,
    )
    ss = [stats] + swaps(stats, bits)

    ins = [kv] + qgs + ss + kv_rims
    layout = {"n_in": len(ins), "count": count, "frames": frames}
    edge = struct(2, tokens, width)
    parts = call(
        functools.partial(backward_kernel, layout, ["r0", "r1"]),
        [edge, edge], ins + [mask_b],
        flops=work, exps=exps, scratch=scratches(4 * PAIRS, 2), limit=14 << 20,
    )
    parts = [exchange(value, side) for side, value in enumerate(parts)]
    full = struct(rows, columns, frames, width)
    ins = ins + [attended, dq]
    layout = {"n_in": len(ins), "count": count, "frames": frames, "held": 2}
    total, attended, dq = call(
        functools.partial(backward_kernel, layout, inner_kinds + edge_kinds),
        [struct(2 * rows, tokens, width, dtype=F32), full, full], ins + [mask_b], to_hbm=(1, 2),
        flops=2 * work, exps=2 * exps, limit=18 << 20,
        scratch=[pltpu.SemaphoreType.DMA((2,))] + scratches(2 * rows * PAIRS, 2),
    )
    dk, dv = call(
        finish_kernel, [full, full], [total] + parts, to_hbm=(0, 1),
        scratch=[pltpu.VMEM(full.shape, BF16)] * 2 + [pltpu.SemaphoreType.DMA((2 * rows,))],
    )
    return back(attended), back(dq), back(dk), back(dv)


def solution(mesh):
    spec = P("frame", "space", None, None)

    return jax.shard_map(
        per_device,
        mesh=mesh,
        in_specs=(spec, spec, spec, spec, P()),
        out_specs=(spec, spec, spec, spec),
        check_vma=False,
    )
```

```python
import functools

import jax
import jax.numpy as jnp
from jax import lax
from jax.experimental import pallas as pl
from jax.experimental.pallas import tpu as pltpu
from jax.sharding import PartitionSpec as P


HEAD_DIM = 64
SCALE = 0.125
NEG = -1e30
PAIR = 2 * HEAD_DIM
PAIRS = 2
PART = PAIRS * PAIR
CHUNK = 16
RING = 4
LOOP_GRAD = False
LOOP_OWN = True
BF16 = jnp.bfloat16
F32 = jnp.float32


def swap(value, bit):
    size = lax.axis_size("frame")
    return lax.ppermute(value, "frame", [(i, i ^ 1 << bit) for i in range(size)])


def swaps(value, bits):
    return [swap(value, bit) for bit in range(bits)]


def exchange(value, side):
    pairs = []
    for low in range(side, lax.axis_size("space") - 1, 2):
        pairs += [(low, low + 1), (low + 1, low)]
    return lax.ppermute(value, "space", pairs)


def struct(*shape, dtype=BF16):
    return jax.ShapeDtypeStruct(shape, dtype)


def call(kernel, outs, ins, flops=0, exps=0, scratch=(), limit=4 << 20, table=None, to_hbm=(), raw=0):
    size = sum(a.size * a.dtype.itemsize for a in ins) + sum(
        o.size * jnp.dtype(o.dtype).itemsize for o in outs
    )
    ins = [pltpu.with_memory_space_constraint(a, pltpu.HBM) for a in ins[:raw]] + [pltpu.with_memory_space_constraint(a, pltpu.VMEM) for a in ins[raw:]]
    specs = [pl.BlockSpec(memory_space=pltpu.HBM if i < raw else pltpu.VMEM) for i in range(len(ins))]
    if table is not None:
        ins = ins + [table]
        specs = specs + [pl.BlockSpec(memory_space=pltpu.SMEM)]
    return pl.pallas_call(
        kernel,
        out_shape=tuple(
            o if i in to_hbm else pltpu.VMEM(o.shape, o.dtype) for i, o in enumerate(outs)
        ),
        in_specs=specs,
        out_specs=tuple(
            pl.BlockSpec(memory_space=pl.ANY if i in to_hbm else pltpu.VMEM) for i in range(len(outs))
        ),
        scratch_shapes=list(scratch),
        compiler_params=pltpu.CompilerParams(vmem_limit_bytes=limit),
        cost_estimate=pl.CostEstimate(flops=flops, bytes_accessed=size, transcendentals=exps),
    )(*ins)


def edge_rows(rows):
    odd = lax.rem(lax.axis_index("space"), 2)
    return (rows - 1) * (1 - odd), (rows - 1) * odd


def pack_kernel(n, *refs):
    sources, (packed, edge0, edge1, *held, sems) = refs[:n], refs[-4 - n :]
    rows, columns, frames, width = sources[0].shape
    flat = (columns * frames, width)
    copies = [
        [pltpu.make_async_copy(source.at[row], held[at].at[row], sems.at[at, row]) for row in range(rows)]
        for at, source in enumerate(sources)
    ]
    for copy in sum(copies, []):
        copy.start()
    for at in range(n):
        for row in range(rows):
            copies[at][row].wait()
            packed[at * rows + row] = held[at][row].reshape(flat)
    for edge, row in zip((edge0, edge1), edge_rows(rows)):
        for at in range(n):
            edge[at] = packed[at * rows + row]


def pack(sources, after=()):
    n = len(sources)
    rows, columns, frames, width = sources[0].shape
    edge = struct(n, columns * frames, width)
    outs = [struct(n * rows, columns * frames, width), edge, edge]
    kernel = functools.partial(pack_kernel, n)
    held = [pltpu.VMEM(s.shape, s.dtype) for s in sources]
    scratch = held + [pltpu.SemaphoreType.DMA((n, rows))]
    return call(kernel, outs, sources + list(after), scratch=scratch, raw=n)


def join_kernel(side0, side1, after, both, keys):
    for side, source in enumerate((side0, side1)):
        both[2 * side] = source[0]
        both[2 * side + 1] = source[1]
        keys[side] = source[0]


def join(sources, after):
    shape = sources[0].shape[1:]
    return call(join_kernel, [struct(4, *shape), struct(2, *shape)], sources + after)


def edge_kernel(*refs):
    sources, targets = refs[:-2], refs[-2:]
    rows = sources[0].shape[0] // 2
    for slot, source in enumerate(sources):
        for target, row in zip(targets, edge_rows(rows)):
            target[slot] = source[rows + row]


def value_edges(sources):
    edge = struct(len(sources), *sources[0].shape[1:])
    return call(edge_kernel, [edge, edge], sources)


def lanes_at(group, pair):
    start = group * PART + pair * PAIR
    if isinstance(group, int):
        return slice(start, start + PAIR)
    return pl.ds(pl.multiple_of(start, PAIR), PAIR)


def over_groups(groups, loop, products, finish):
    if loop:

        def step(group, _):
            products(group)
            finish(group)
            return 0

        lax.fori_loop(0, groups, step, 0)
        return
    products(0)
    for group in range(groups):
        if group + 1 < groups:
            products(group + 1)
        finish(group)


def head_rows(value, lane_head):
    zero = jnp.zeros_like(value)
    return jnp.concatenate([jnp.where(lane_head == h, value, zero) for h in range(2)], axis=0)


def head_lanes(stacked, lane_head):
    tokens = stacked.shape[0] // 2
    return jnp.where(lane_head == 0, stacked[:tokens], stacked[tokens:])


def nt(a, b):
    return lax.dot_general(a, b, (((1,), (1,)), ((), ())), preferred_element_type=F32)


def nn(a, b):
    return jnp.dot(a, b, preferred_element_type=F32)


class Pieces:
    def __init__(self, refs, rows, mids, rim_slots):
        self.rows = rows
        self.mids = [(refs[i], s) for i, s in mids]
        self.rims = [[(refs[i], s) for i, s in side] for side in rim_slots]

    def window(self, kind, lanes):
        out = []
        for at in range(3):
            for block, (mid, base) in enumerate(self.mids):
                if isinstance(kind, int):
                    out.append(mid[base + kind - 1 + at, :, lanes])
                elif at == 0:
                    ref, slot = self.rims[int(kind)][block]
                    out.append(ref[slot, :, lanes])
                else:
                    edge = edge_rows(self.rows)[int(kind)]
                    inner = jnp.where(edge == 0, 1, edge - 1)
                    out.append(mid[base + (edge if at == 1 else inner), :, lanes])
        return jnp.concatenate(out, axis=0)


def row_of(kind, rows):
    return kind if isinstance(kind, int) else edge_rows(rows)[int(kind)]


def rim_open(side):
    band, size = lax.axis_index("space"), lax.axis_size("space")
    odd = lax.rem(band, 2)
    up = (odd == 0) if side == 0 else (odd == 1)
    other = jnp.where(up, band + 1, band - 1)
    return (other >= 0) & (other < size)


def build_masks(mask_ref, blocks, frames, table, queries_here):
    shape = mask_ref.shape[1:]
    tokens = shape[1] // blocks
    lane = lax.broadcasted_iota(jnp.int32, shape, 1)
    sub = lax.broadcasted_iota(jnp.int32, shape, 0)
    bad = NEG if queries_here else -NEG
    which = sub if queries_here else lane
    which = lax.rem(which, frames)
    group = lane // tokens
    here = lax.axis_index("frame")
    value = jnp.zeros(shape, F32)
    for block in range(1, blocks):
        owner = here if queries_here else jnp.bitwise_xor(here, 1 << (block - 1))
        for frame in range(frames):
            off = jnp.where(table[block - 1, owner * frames + frame] == 1, 0.0, bad)
            value = jnp.where((group == block) & (which == frame), off.astype(F32), value)
    mask_ref[0] = value
    if queries_here:
        for side in range(2):
            mask_ref[1 + side] = value + jnp.where(rim_open(side), 0.0, bad).astype(F32)


def mask_kernel(blocks, frames, after, table, mask_f, mask_b):
    build_masks(mask_f, blocks, frames, table, True)
    build_masks(mask_b, blocks, frames, table, False)


def forward_kernel(layout, kinds, carried, *refs):
    qg = refs[layout["own"]]
    rows = qg.shape[0] // 2
    keys, values = (Pieces(refs, rows, *layout[name]) for name in ("k", "v"))
    n_in = layout["n_in"]
    mask = refs[n_in]
    out, dq, stats = refs[n_in + 1 :][:3]
    s_scr, d_scr, p_scr, _ = refs[-4:]
    tokens, width = qg.shape[1:]
    columns, frames = out.shape[1:3]
    if carried:
        for target, source in zip((out, dq), refs[n_in - 3 : n_in - 1]):
            for at, row in enumerate(carried):
                target[row] = source[at]
        for at in range(len(carried)):
            stats[at] = refs[n_in - 1][at]
    lane_head = lax.broadcasted_iota(jnp.int32, (tokens, PAIR), 1) // HEAD_DIM
    lane = lax.broadcasted_iota(jnp.int32, (2 * tokens, 128), 1)
    slot_of = lambda row: row if carried else row - 1
    units = [(slot, pair) for slot in range(len(kinds)) for pair in range(PAIRS)]

    def step(group, _):
        starts = [pl.multiple_of(group * PART + pair * PAIR, PAIR) for pair in range(PAIRS)]
        lanes_of = [pl.ds(start, PAIR) for start in starts]
        for unit, (slot, pair) in enumerate(units):
            lanes, kind = lanes_of[pair], kinds[slot]
            row = row_of(kind, rows)
            s_scr[unit] = nt(head_rows(qg[row, :, lanes] * SCALE, lane_head), keys.window(kind, lanes))
            d_scr[unit] = nt(head_rows(qg[rows + row, :, lanes], lane_head), values.window(kind, lanes))
        tops, totals = [], []
        for unit, (slot, pair) in enumerate(units):
            top_parts, total_parts = [], []
            first = mask[0] if isinstance(kinds[slot], int) else mask[1 + int(kinds[slot])]
            bias = jnp.concatenate([first, mask[0], mask[0]], axis=1)
            bias = jnp.concatenate([bias] * (CHUNK // 8), axis=0)
            for start in range(0, 2 * tokens, CHUNK):
                scores = s_scr[unit, start : start + CHUNK, :] + bias
                top = jnp.max(scores, axis=1, keepdims=True)
                raw = jnp.exp(scores - top)
                s_scr[unit, start : start + CHUNK, :] = raw
                p_scr[unit, start : start + CHUNK, :] = raw.astype(BF16)
                top_parts.append(top)
                total_parts.append(jnp.sum(raw, axis=1, keepdims=True))
            tops.append(jnp.concatenate(top_parts, axis=0))
            totals.append(jnp.concatenate(total_parts, axis=0))
        cols = jnp.zeros((2 * tokens, 128), F32)
        deltas, scales = [], []
        for unit, (slot, pair) in enumerate(units):
            lanes, kind = lanes_of[pair], kinds[slot]
            row = row_of(kind, rows)
            scale = 1.0 / totals[unit]
            wide = nn(p_scr[unit], values.window(kind, lanes)) * scale
            attended = head_lanes(wide, lane_head).astype(BF16)
            out[slot_of(row), :, :, lanes] = attended.reshape(columns, frames, PAIR)
            prod = qg[rows + row, :, lanes].astype(F32) * attended.astype(F32)
            delta = jnp.sum(head_rows(prod, lane_head), axis=1, keepdims=True)
            deltas.append(delta)
            scales.append(scale)
            cols = jnp.where(lane == 2 * unit, tops[unit] + jnp.log(totals[unit]), cols)
            cols = jnp.where(lane == 2 * unit + 1, delta, cols)
        for unit, (slot, pair) in enumerate(units):
            for start in range(0, 2 * tokens, CHUNK):
                part = slice(start, start + CHUNK)
                grad_scores = s_scr[unit, part, :] * (d_scr[unit, part, :] - deltas[unit][part])
                p_scr[unit, part, :] = grad_scores.astype(BF16)
        for unit, (slot, pair) in enumerate(units):
            lanes, kind = lanes_of[pair], kinds[slot]
            wide = nn(p_scr[unit], keys.window(kind, lanes)) * (scales[unit] * SCALE)
            grad_q = head_lanes(wide, lane_head).astype(BF16)
            dq[slot_of(row_of(kind, rows)), :, :, lanes] = grad_q.reshape(columns, frames, PAIR)
        turned = cols.T
        for unit, (slot, pair) in enumerate(units):
            for which in range(2):
                line = turned[2 * unit + which : 2 * unit + which + 1]
                for h in range(2):
                    to = which * 2 * PAIRS + pair * 2 + h
                    stats[len(carried) + slot, group, to : to + 1, :] = line[:, h * tokens : (h + 1) * tokens]
        return 0

    lax.fori_loop(0, width // PART, step, 0)


def forward_edge_kernel(layout, kinds, carried, *refs):
    qg = refs[layout["own"]]
    rows = qg.shape[0] // 2
    keys, values = (Pieces(refs, rows, *layout[name]) for name in ("k", "v"))
    n_in = layout["n_in"]
    mask = refs[n_in]
    out, stats, raw_out, column_out = refs[n_in + 1 :][:4]
    s_scr, p_scr = refs[-2:]
    tokens, width = qg.shape[1:]
    columns, frames = out.shape[1:3]
    if carried:
        for at, row in enumerate(carried):
            out[row] = refs[n_in - 2][at]
            stats[at] = refs[n_in - 1][at]
    lane_head = lax.broadcasted_iota(jnp.int32, (tokens, PAIR), 1) // HEAD_DIM
    lane = lax.broadcasted_iota(jnp.int32, (2 * tokens, 128), 1)
    slot_of = lambda row: row if carried else row - 1
    units = [(slot, pair) for slot in range(len(kinds)) for pair in range(PAIRS)]

    def step(group, _):
        starts = [pl.multiple_of(group * PART + pair * PAIR, PAIR) for pair in range(PAIRS)]
        lanes_of = [pl.ds(start, PAIR) for start in starts]
        for unit, (slot, pair) in enumerate(units):
            lanes, kind = lanes_of[pair], kinds[slot]
            row = row_of(kind, rows)
            s_scr[unit] = nt(head_rows(qg[row, :, lanes] * SCALE, lane_head), keys.window(kind, lanes))
        tops, totals = [], []
        for unit, (slot, pair) in enumerate(units):
            top_parts, total_parts = [], []
            first = mask[0] if isinstance(kinds[slot], int) else mask[1 + int(kinds[slot])]
            bias = jnp.concatenate([first, mask[0], mask[0]], axis=1)
            bias = jnp.concatenate([bias] * (CHUNK // 8), axis=0)
            for start in range(0, 2 * tokens, CHUNK):
                scores = s_scr[unit, start : start + CHUNK, :] + bias
                top = jnp.max(scores, axis=1, keepdims=True)
                raw = jnp.exp(scores - top)
                raw_out[group * len(units) + unit, start : start + CHUNK, :] = raw
                p_scr[unit, start : start + CHUNK, :] = raw.astype(BF16)
                top_parts.append(top)
                total_parts.append(jnp.sum(raw, axis=1, keepdims=True))
            tops.append(jnp.concatenate(top_parts, axis=0))
            totals.append(jnp.concatenate(total_parts, axis=0))
        cols = jnp.zeros((2 * tokens, 128), F32)
        for unit, (slot, pair) in enumerate(units):
            lanes, kind = lanes_of[pair], kinds[slot]
            row = row_of(kind, rows)
            scale = 1.0 / totals[unit]
            wide = nn(p_scr[unit], values.window(kind, lanes)) * scale
            attended = head_lanes(wide, lane_head).astype(BF16)
            out[slot_of(row), :, :, lanes] = attended.reshape(columns, frames, PAIR)
            prod = qg[rows + row, :, lanes].astype(F32) * attended.astype(F32)
            delta = jnp.sum(head_rows(prod, lane_head), axis=1, keepdims=True)
            for which, column in enumerate((scale, delta)):
                column_out[group * len(units) + unit, which] = jnp.broadcast_to(column, (2 * tokens, 128))
            cols = jnp.where(lane == 2 * unit, tops[unit] + jnp.log(totals[unit]), cols)
            cols = jnp.where(lane == 2 * unit + 1, delta, cols)
        turned = cols.T
        for unit, (slot, pair) in enumerate(units):
            for which in range(2):
                line = turned[2 * unit + which : 2 * unit + which + 1]
                for h in range(2):
                    to = which * 2 * PAIRS + pair * 2 + h
                    stats[len(carried) + slot, group, to : to + 1, :] = line[:, h * tokens : (h + 1) * tokens]
        return 0

    lax.fori_loop(0, width // PART, step, 0)


def forward_grad_kernel(layout, kinds, carried, *refs):
    qg = refs[layout["own"]]
    rows = qg.shape[0] // 2
    keys, values = (Pieces(refs, rows, *layout[name]) for name in ("k", "v"))
    n_in = layout["n_in"]
    inner_dq, raw_in, column_in = refs[n_in - 3 : n_in]
    dq, d_scr, p_scr = refs[n_in:]
    tokens, width = qg.shape[1:]
    columns, frames = dq.shape[1:3]
    window = d_scr.shape[2]
    for at, row in enumerate(carried):
        dq[row] = inner_dq[at]
    lane_head = lax.broadcasted_iota(jnp.int32, (tokens, PAIR), 1) // HEAD_DIM
    units = [(slot, pair) for slot in range(len(kinds)) for pair in range(PAIRS)]

    def products(group):
        for unit, (slot, pair) in enumerate(units):
            lanes, kind = lanes_at(group, pair), kinds[slot]
            row = row_of(kind, rows)
            at = (0 if layout["loop"] else group % 2) * len(units) + unit
            d_scr[at] = nt(head_rows(qg[rows + row, :, lanes], lane_head), values.window(kind, lanes))

    def finish(group):
        base = (0 if layout["loop"] else group % 2) * len(units)
        for unit, (slot, pair) in enumerate(units):
            held = group * len(units) + unit
            for start in range(0, 2 * tokens, CHUNK):
                part = slice(start, start + CHUNK)
                delta = column_in[held, 1, part, :]
                for low in range(0, window, 128):
                    size = min(128, window - low)
                    span = slice(low, low + size)
                    value = raw_in[held, part, span] * (d_scr[base + unit, part, span] - delta[:, :size])
                    p_scr[base + unit, part, span] = value.astype(BF16)
        for unit, (slot, pair) in enumerate(units):
            lanes, kind = lanes_at(group, pair), kinds[slot]
            scale = column_in[group * len(units) + unit, 0] * SCALE
            wide = nn(p_scr[base + unit], keys.window(kind, lanes)) * scale
            grad_q = head_lanes(wide, lane_head).astype(BF16)
            dq[row_of(kind, rows), :, :, lanes] = grad_q.reshape(columns, frames, PAIR)

    over_groups(width // PART, layout["loop"], products, finish)


def backward_kernel(layout, kinds, *refs):
    n_in, count = layout["n_in"], layout["count"]
    kv = refs[0]
    qgs, stats_of = refs[1 : 1 + count], refs[1 + count : 1 + 2 * count]
    rims = refs[1 + 2 * count : n_in]
    mask, *outs = refs[n_in:-4]
    s_scr, d_scr, p_scr, t_scr = refs[-4:]
    rows = kv.shape[0] // 2
    copies = []
    if layout.get("held"):
        sems = refs[-5]
        for at, (held, out) in enumerate(zip(refs[n_in - 2 : n_in], outs[1:3])):
            copies.append(pltpu.make_async_copy(held, out, sems.at[at]))
            copies[-1].start()
    tokens, width = kv.shape[1:]
    part = count * tokens
    lane_head = lax.broadcasted_iota(jnp.int32, (tokens, PAIR), 1) // HEAD_DIM
    units = [(kind, pair) for kind in kinds for pair in range(PAIRS)]

    def query_rows(kind):
        inner = rows - 2
        if isinstance(kind, int):
            first, _ = edge_rows(rows)
            out = []
            for row in (kind - 1, kind, kind + 1):
                if 0 < row < rows - 1:
                    out.append((row, row - 1))
                else:
                    out.append((row, jnp.where(first == row, inner, inner + 1)))
            return out
        side = int(kind[-1])
        edge = edge_rows(rows)[side]
        if kind[0] == "r":
            return [(edge, inner + side)]
        near = jnp.where(edge == 0, 1, edge - 1)
        return [(edge, inner + side), (near, near - 1)]

    def key_rows(kind, tensor, lanes):
        if isinstance(kind, int):
            return kv[tensor * rows + kind, :, lanes]
        side = int(kind[-1])
        if kind[0] == "r":
            return rims[side][tensor, :, lanes]
        return kv[tensor * rows + edge_rows(rows)[side], :, lanes]

    def window(kind, tensor, lanes):
        found = [qg[tensor * rows + row, :, lanes] for row, _ in query_rows(kind) for qg in qgs]
        return jnp.concatenate(found, axis=0)

    def products(group):
        for unit, (kind, pair) in enumerate(units):
            lanes = lanes_at(group, pair)
            size = len(query_rows(kind)) * part
            at = (0 if layout["loop"] else group % 2) * len(units) + unit
            s_scr[at, :, :size] = nt(
                head_rows(key_rows(kind, 0, lanes) * SCALE, lane_head), window(kind, 0, lanes)
            )
            d_scr[at, :, :size] = nt(
                head_rows(key_rows(kind, 1, lanes), lane_head), window(kind, 1, lanes)
            )

    def finish(group):
        base = (0 if layout["loop"] else group % 2) * len(units)
        stats = {
            kind: jnp.concatenate(
                [ref[slot, group] for _, slot in query_rows(kind) for ref in stats_of], axis=1
            )
            for kind in kinds
        }
        for unit, (kind, pair) in enumerate(units):
            stat = stats[kind]
            size = stat.shape[1]
            bias = jnp.concatenate([mask[0, 0:1]] * (size // part), axis=1)
            for h in range(2):
                at = pair * 2 + h
                lse = stat[at : at + 1] + bias
                delta = stat[2 * PAIRS + at : 2 * PAIRS + at + 1]
                for start in range(h * tokens, (h + 1) * tokens, CHUNK):
                    rows_at = slice(start, start + CHUNK)
                    probs = jnp.exp(s_scr[base + unit, rows_at, :size] - lse)
                    p_scr[base + unit, rows_at, :size] = probs.astype(BF16)
                    grad_scores = probs * (d_scr[base + unit, rows_at, :size] - delta)
                    t_scr[base + unit, rows_at, :size] = grad_scores.astype(BF16)
        for unit, (kind, pair) in enumerate(units):
            lanes = lanes_at(group, pair)
            size = len(query_rows(kind)) * part
            grad_v = head_lanes(nn(p_scr[base + unit, :, :size], window(kind, 1, lanes)), lane_head)
            grad_k = head_lanes(nn(t_scr[base + unit, :, :size], window(kind, 0, lanes)), lane_head) * SCALE
            for tensor, value in enumerate((grad_k, grad_v)):
                if isinstance(kind, str) and kind[0] == "r":
                    outs[int(kind[-1])][tensor, :, lanes] = value.astype(BF16)
                else:
                    row = row_of(kind, rows)
                    outs[0][tensor * rows + row, :, lanes] = value

    over_groups(width // PART, layout["loop"], products, finish)
    for copy in copies:
        copy.wait()


def finish_kernel(total, part0, part1, dk, dv, dk_held, dv_held, sems):
    rows, columns, frames, width = dk.shape
    copies = []

    def send(tensor, row, value):
        held, out = ((dk_held, dk), (dv_held, dv))[tensor]
        held[row] = value.astype(BF16).reshape(columns, frames, width)
        copies.append(pltpu.make_async_copy(held.at[row], out.at[row], sems.at[len(copies)]))
        copies[-1].start()

    for tensor in range(2):
        for row in range(1, rows - 1):
            send(tensor, row, total[tensor * rows + row])
        for part, row in zip((part0, part1), edge_rows(rows)):
            send(tensor, row, total[tensor * rows + row] + part[tensor].astype(F32))
    for copy in copies:
        copy.wait()


def per_device(query_vectors, key_vectors, value_vectors, out_cotangent, partner_mask):
    frames, rows, columns, width = query_vectors.shape
    bits = min(4, lax.axis_size("frame").bit_length() - 1)
    count = bits + 1
    tokens = frames * columns
    groups = width // PART
    window = 3 * count * tokens
    table = partner_mask.T
    turn = lambda a: jnp.transpose(a, (1, 2, 0, 3))
    back = lambda a: jnp.transpose(a, (2, 0, 1, 3))

    kv, kv_edge0, kv_edge1 = pack([turn(key_vectors), turn(value_vectors)])
    kvs = [kv] + swaps(kv, bits)
    kv_rims = [exchange(kv_edge0, 0), exchange(kv_edge1, 1)]
    mask = lambda n: struct(n, 8, count * tokens, dtype=F32)
    mask_f, mask_b = call(functools.partial(mask_kernel, count, frames), [mask(3), mask(1)], [kv_edge0], table=table)
    joined, k_joined = join(kv_rims, [mask_b])
    core_rims = swap(joined, 0)
    k_rims_of = [swap(k_joined, bit) for bit in range(1, bits)]
    qg, _, _ = pack([turn(query_vectors), turn(out_cotangent)], [kv_edge0])
    qgs = [qg] + swaps(qg, bits)
    v_far = [exchange(e, side) for side, e in enumerate(value_edges(kvs[2:]))]

    inner_kinds = list(range(1, rows - 1))
    edge_kinds = ["0", "1"]
    inner = len(inner_kinds)
    work = 4 * 2 * (width // PAIR) * 2 * tokens * window * PAIR
    exps = (width // HEAD_DIM) * tokens * window
    line = lambda n: struct(n, columns, frames, width)

    def scratches(n, extra):
        wide = [pltpu.VMEM((n, 2 * tokens, window), F32)] * 2
        return wide + [pltpu.VMEM((n, 2 * tokens, window), BF16)] * extra

    def gathered(at, rim_at, tensor):
        mids = [(at + block, tensor * rows) for block in range(count)]
        if rim_at is None:
            return mids, []
        sides = []
        for side in range(2):
            near = [(rim_at + side, tensor), (rim_at + 2, 2 * side + tensor)]
            if tensor == 0:
                far = [(rim_at + 3 + at, side) for at in range(bits - 1)]
            else:
                far = [(rim_at + 2 + bits + side, at) for at in range(bits - 1)]
            sides.append(near + far)
        return mids, sides

    stat = lambda n: struct(n, groups, 4 * PAIRS, tokens, dtype=F32)
    ins = [qg] + kvs
    layout = {"n_in": len(ins), "own": 0, "k": gathered(1, None, 0), "v": gathered(1, None, 1)}
    inner_out = call(
        functools.partial(forward_kernel, layout, inner_kinds, ()),
        [line(inner), line(inner), stat(inner)], ins + [mask_f],
        flops=work * inner, exps=exps * inner, scratch=scratches(RING, 2), limit=14 << 20,
    )
    rim_at = len(ins)
    inner_att, inner_dq, inner_stats = inner_out
    base = ins + kv_rims + [core_rims] + k_rims_of + v_far
    found = {"own": 0, "k": gathered(1, rim_at, 0), "v": gathered(1, rim_at, 1)}
    ins = base + [inner_att, inner_stats]
    layout = {"n_in": len(ins), **found}
    jobs = groups * PAIRS * 2
    kept = [struct(jobs, 2 * tokens, window, dtype=F32), struct(jobs, 2, 2 * tokens, 128, dtype=F32)]
    piece = lambda n, dtype: pltpu.VMEM((n, 2 * tokens, window), dtype)
    attended, stats, *kept = call(
        functools.partial(forward_edge_kernel, layout, edge_kinds, inner_kinds),
        [line(rows), stat(rows)] + kept, ins + [mask_f],
        flops=work, exps=exps * 2, scratch=[piece(2 * PAIRS, F32), piece(2 * PAIRS, BF16)], limit=10 << 20,
    )
    ins = base + [inner_dq] + kept
    layout = {"n_in": len(ins), "loop": LOOP_GRAD, **found}
    (dq,) = call(
        functools.partial(forward_grad_kernel, layout, edge_kinds, inner_kinds),
        [line(rows)], ins,
        flops=work, scratch=[piece(4 * PAIRS, F32), piece(4 * PAIRS, BF16)], limit=10 << 20,
    )
    ss = [stats] + swaps(stats, bits)

    ins = [kv] + qgs + ss + kv_rims
    layout = {"n_in": len(ins), "count": count, "loop": False}
    edge = struct(2, tokens, width)
    parts = call(
        functools.partial(backward_kernel, layout, ["r0", "r1"]),
        [edge, edge], ins + [mask_b],
        flops=work, exps=exps, scratch=scratches(4 * PAIRS, 2), limit=14 << 20,
    )
    parts = [exchange(value, side) for side, value in enumerate(parts)]
    full = struct(rows, columns, frames, width)
    ins = ins + [attended, dq]
    layout = {"n_in": len(ins), "count": count, "loop": LOOP_OWN, "held": 2}
    total, attended, dq = call(
        functools.partial(backward_kernel, layout, inner_kinds + edge_kinds),
        [struct(2 * rows, tokens, width, dtype=F32), full, full], ins + [mask_b], to_hbm=(1, 2),
        flops=2 * work, exps=2 * exps, limit=18 << 20,
        scratch=[pltpu.SemaphoreType.DMA((2,))] + scratches(2 * rows * PAIRS, 2),
    )
    dk, dv = call(
        finish_kernel, [full, full], [total] + parts, to_hbm=(0, 1),
        scratch=[pltpu.VMEM(full.shape, BF16)] * 2 + [pltpu.SemaphoreType.DMA((2 * rows,))],
    )
    return back(attended), back(dq), back(dk), back(dv)


def solution(mesh):
    spec = P("frame", "space", None, None)

    return jax.shard_map(
        per_device,
        mesh=mesh,
        in_specs=(spec, spec, spec, spec, P()),
        out_specs=(spec, spec, spec, spec),
        check_vma=False,
    )
```
